32 devices in a mesh: parts: 2 (over x), space: 16 (over z, y, core).
Axes of the slice: x: 2, y: 2, z: 4, core: 2. Of those that a mesh axis runs over, the one named last changes fastest.
Arguments:
- images: bfloat16 [8, 32, 128, 512], P('parts', 'space'), parts along dimension 0, may hold values from 0 to 0.099609375
- target: bfloat16 [8, 16, 64, 1024], P('parts', 'space'), parts along dimension 0, may hold values from -8 to 8
- raw_filters: bfloat16 [2048, 3, 3, 512], P(('parts', 'space')), parts along dimension 0, may hold values from -39 to 39
Outputs:
- input_grads: bfloat16 [8, 32, 128, 512], P('parts', 'space'), parts along dimension 0
- filter_grads: float32 [2048, 3, 3, 512], P(('parts', 'space')), parts along dimension 0
The draws below stay inside these ranges and needn't reach their ends.
There are 2 independent parts, one for each index of `parts`. The reference program is written for one: setup_inputs(seed, part) draws one part's arguments, and reference() takes and returns one part's arrays. A program takes and returns all parts, laid end to end along the dimension named above; each array names one. Nothing has to cross between parts.
All inputs are finite; a program needn't handle non-finite values.
Results may differ from the reference program's by a relative error of at most 0.008.
Values may be sent and summed in bfloat16 or wider, within the bound.
A program may use at most 128 MiB of HBM per device.

```python
import math
import jax
import jax.numpy as jnp
from jax import lax

CIN = 512
COUT = 1024
IMG = 4
WO = 64
OUT_ROWS = 16
IN_ROWS = 32
IN_COLS = 128


def draw_raw_filters(key, part):
    keys = jax.random.split(key, 4)
    shape = (COUT, 3, 3, CIN)
    noise = jax.random.truncated_normal(keys[0], -4.0, 4.0, shape, jnp.float32)
    row_scale = jnp.exp(jax.random.uniform(keys[1], (COUT, 1, 1, 1), jnp.float32, math.log(0.3), math.log(3.0)))
    col_scale = jnp.exp(jax.random.uniform(keys[2], (1, 1, 1, CIN), jnp.float32, math.log(0.3), math.log(3.0)))
    offset = jax.random.uniform(keys[3], (COUT, 1, 1, 1), jnp.float32, -1.0, 1.0) * row_scale
    return (noise * row_scale * col_scale + offset).astype(jnp.bfloat16)


def level_of(own_key, extent, cuts, smallest, top_value):
    def one(position, shards_of):
        draws = jax.random.uniform(jax.random.fold_in(jax.random.fold_in(own_key, 6), position), (shards_of,), jnp.float32, smallest / len(cuts), top_value / len(cuts))
        return jnp.repeat(jnp.exp(draws), extent[position] // shards_of).reshape((-1,) + (1,) * (len(extent) - position - 1))

    gain = one(*cuts[0])
    for cut in cuts[1:]:
        gain = gain * one(*cut)
    return gain


def gaussian(own_key, dims, scale, limit, cuts=(), kind=jnp.bfloat16):
    gain = level_of(own_key, dims, cuts, -0.22, 0.18) if cuts else 1.0
    entries = jax.random.normal(own_key, dims, jnp.float32) * scale * gain
    return jnp.minimum(jnp.maximum(entries, -limit), limit).astype(kind)


def setup_inputs(seed: int = 0, part: int = 0) -> dict:
    key_of = jax.random.split(jax.random.key(seed), 4)
    part_keys = jax.random.split(jax.random.fold_in(key_of[3], part), 4)
    images = jnp.clip(0.099609375 * jax.random.uniform(part_keys[0], (IMG, IN_ROWS, IN_COLS, CIN), jnp.float32) ** level_of(part_keys[0], (IMG, IN_ROWS, IN_COLS, CIN), ((1, 16),), -0.2, 0.2), 0.0, 0.099609375).astype(jnp.bfloat16)
    target = gaussian(part_keys[1], (IMG, OUT_ROWS, WO, COUT), 2.0, 8.0, ((1, 16),))
    raw_filters = draw_raw_filters(jax.random.fold_in(jax.random.fold_in(key_of[3], part), 71), part)
    return dict(images=images, target=target, raw_filters=raw_filters)


EPS = 1e-05
GRAD_SCALE = 0.015625

def extract(padded):
    pieces = []
    for kh in range(3):
        for kw in range(3):
            pieces.append(padded[:, kh:kh + 2 * OUT_ROWS:2, kw:kw + 2 * WO:2, :])
    return jnp.concatenate(pieces, axis=-1)

def reference(images, target, raw_filters):
    weights = raw_filters.astype(jnp.float32).reshape(COUT, 9 * CIN)
    mean_w = lax.optimization_barrier(jnp.mean(weights, axis=1, keepdims=True))
    centered = weights - mean_w
    std_w = jnp.sqrt(lax.optimization_barrier(jnp.mean(centered * centered, axis=1, keepdims=True)) + EPS)
    w_hat = centered / std_w
    w_bf = w_hat.astype(jnp.bfloat16)
    padded = jnp.pad(images, ((0, 0), (1, 1), (1, 1), (0, 0)))
    patches = extract(padded).reshape(IMG * OUT_ROWS * WO, 9 * CIN)
    outputs = jnp.dot(patches, w_bf.T, preferred_element_type=jnp.float32)
    wanted = target.reshape(IMG * OUT_ROWS * WO, COUT).astype(jnp.float32)
    grad_y = ((outputs - wanted) * GRAD_SCALE).astype(jnp.bfloat16)
    summed = jnp.dot(grad_y.T, patches, preferred_element_type=jnp.float32)
    first_mean = lax.optimization_barrier(jnp.mean(summed, axis=1, keepdims=True))
    second_mean = lax.optimization_barrier(jnp.mean(summed * w_hat, axis=1, keepdims=True))
    filter_grads = ((summed - first_mean - w_hat * second_mean) / std_w).reshape(COUT, 3, 3, CIN)
    columns = jnp.dot(grad_y, w_bf, preferred_element_type=jnp.float32)
    columns = columns.reshape(IMG, OUT_ROWS, WO, 9 * CIN)
    start_field = jnp.zeros(padded.shape, jnp.float32)
    unused, backward = jax.vjp(extract, start_field)
    spread_back = backward(columns)[0]
    input_grads = spread_back[:, 1:-1, 1:-1, :].astype(jnp.bfloat16)
    return (input_grads, filter_grads)
```

```python
import functools

import jax
import jax.numpy as jnp
from jax import lax
from jax.experimental import pallas as pl
from jax.experimental.pallas import tpu as pltpu
from jax.sharding import PartitionSpec as P

EPS = 1e-05
GRAD_SCALE = 0.015625
WIDE = 4
PIECES = 3
F32 = jnp.float32
BF = jnp.bfloat16
NT = (((1,), (1,)), ((), ()))
NN = (((1,), (0,)), ((), ()))
TN = (((0,), (0,)), ((), ()))
MESH = pl.DeviceIdType.MESH


def dot(a, b, dims):
    return lax.dot_general(a, b, dims, preferred_element_type=F32)


def kernel(
    tall, own, half, cin,
    images, target, filters_in, dout, gout,
    raw, rim_raw, goal_raw, wraw, stat,
    x, xt, w, goal, tg, gy, gys, gt, gts, g, part_in, part_out,
    to_p, from_p, to_q, from_q, acc, rim_s, rim_p, rim_q, rim_z,
    l_sem, i_recv, i_send, w_recv, w_send, t_recv, t_send, r_recv, r_send,
    g_recv, g_send, d_recv, d_send, e_recv, e_send,
):
    me = lax.axis_index("space")
    r, f = me // WIDE, me % WIDE
    base = r * WIDE
    fp = f + 1 - 2 * (f % 2)
    fq = f + 2 - 4 * (f // 2)
    fd = fp + 2 - 4 * (fp // 2)
    p, q, d = base + fp, base + fq, base + fd
    above, below = me - WIDE, me + WIDE
    imgs = images.shape[0]
    px = imgs * half
    two, one = 2 * cin, cin
    three = 3 * cin
    filters = tall * own
    fan = 9 * cin
    mid = tall // 2
    hf = filters // 2
    flip = r // mid
    u = r + flip * (tall - 1 - 2 * r)
    ahead_dev = me + WIDE - 2 * WIDE * flip
    behind_dev = me - WIDE + 2 * WIDE * flip
    at_end = u == 0
    inside = u > 0

    def rc(src, dst, ssem, rsem, to):
        return pltpu.make_async_remote_copy(
            src_ref=src, dst_ref=dst, send_sem=ssem, recv_sem=rsem,
            device_id={"space": to}, device_id_type=MESH,
        )

    def wait_in(dst, rsem):
        rc(dst, dst, rsem, rsem, p).wait_recv()

    def rows_of(b):
        return pl.ds(pl.multiple_of(b * own, own), own)

    wide_cols = fan // PIECES

    def cols_of(k):
        return slice(k * wide_cols, (k + 1) * wide_cols)

    def block(n):
        return n + flip * (tall - 1 - 2 * n)

    def nth(i):
        near = jnp.where(i % 2 == 1, u + (i + 1) // 2, u - i // 2)
        return jnp.where(i > 2 * u, i, near)

    bar = pltpu.get_barrier_semaphore()

    def greet(to):
        pl.semaphore_signal(bar, inc=1, device_id={"space": to}, device_id_type=MESH)

    for to in (p, q, d):
        greet(to)

    @pl.when(r > 0)
    def _():
        greet(above)

    @pl.when(r < tall - 1)
    def _():
        greet(below)

    load_w = pltpu.make_async_copy(filters_in, wraw, l_sem.at[0])
    load_x = pltpu.make_async_copy(images, raw.at[f], l_sem.at[1])
    load_t = pltpu.make_async_copy(target, goal_raw, l_sem.at[2])
    load_w.start()
    load_x.start()
    load_t.start()

    @pl.when(inside)
    def _():
        pl.semaphore_wait(bar, 5)

    @pl.when(at_end)
    def _():
        pl.semaphore_wait(bar, 4)

    pairs = 2
    per = imgs // pairs
    order = [(row, h) for row in (1, 0) for h in range(pairs)]

    def piece_of(ref, j):
        row, h = order[j]
        return ref.at[slice(h * per, (h + 1) * per), row]

    def img_copy(j, k, to):
        return rc(piece_of(images, j), piece_of(raw.at[f], j), i_send.at[k, j], i_recv.at[f, j], to)

    def fwd_copy(j):
        slot = piece_of(raw.at[fq], j)
        return rc(slot, slot, i_send.at[2, j], i_recv.at[fq, j], p)

    def img_wait(t, j):
        wait_in(piece_of(raw.at[t], j), i_recv.at[t, j])

    rim_in = rc(images.at[:, 1], rim_raw, r_send.at[0], r_recv, below)
    rim_to_p = rc(rim_raw, rim_raw, r_send.at[1], r_recv, p)
    rim_to_q = rc(rim_raw, rim_raw, r_send.at[2], r_recv, q)

    for j in range(len(order)):
        img_copy(j, 1, q).start()

    @pl.when((f == 3) & (r < tall - 1))
    def _():
        rim_in.start()

    def w_copy(b, k, way):
        slot = w.at[rows_of(b), cols_of(k)]
        to = below if way == 0 else above
        return rc(slot, slot, w_send.at[way, b, k], w_recv.at[b, k], to)

    load_w.wait()
    centre = wraw[0].astype(F32)
    for k in range(1, 9):
        centre += wraw[k].astype(F32)
    centre = jnp.sum(centre, axis=1, keepdims=True) * (1.0 / fan)
    spread = jnp.zeros((own, cin), F32)
    for k in range(9):
        off = wraw[k].astype(F32) - centre
        spread += off * off
    spread = jnp.sqrt(jnp.sum(spread, axis=1, keepdims=True) * (1.0 / fan) + EPS)
    inv = 1.0 / spread
    stat[0] = jnp.broadcast_to(centre, (own, 128))
    stat[1] = jnp.broadcast_to(inv, (own, 128))
    taps_per = 9 // PIECES
    for k in range(PIECES):
        for n in range(k * taps_per, (k + 1) * taps_per):
            w[rows_of(r), n * cin : (n + 1) * cin] = ((wraw[n].astype(F32) - centre) * inv).astype(BF)

        @pl.when(r < tall - 1)
        def _():
            w_copy(r, k, 0).start()

        @pl.when(r > 0)
        def _():
            w_copy(r, k, 1).start()

    for j in range(len(order)):
        img_copy(j, 0, p).start()

    def pass_on(s, k):
        up, dn = r - s, r + s

        @pl.when(inside & (up >= 0))
        def _():
            wait_in(w.at[rows_of(up), cols_of(k)], w_recv.at[up, k])
            w_copy(up, k, 0).start()

        @pl.when(inside & (dn <= tall - 1))
        def _():
            wait_in(w.at[rows_of(dn), cols_of(k)], w_recv.at[dn, k])
            w_copy(dn, k, 1).start()

    def w_wait_end(b):
        @pl.when(at_end)
        def _():
            for k in range(PIECES):
                wait_in(w.at[rows_of(b), cols_of(k)], w_recv.at[b, k])

    load_t.wait()
    want = goal_raw[...].reshape(px, goal_raw.shape[2])
    wide = goal_raw.shape[2]
    line = lax.broadcasted_iota(jnp.int32, (filters, wide), 0)
    chan = lax.broadcasted_iota(jnp.int32, (filters, wide), 1)
    first = (line // own) * (own * WIDE) + line % own
    for t in range(WIDE):
        pick = jnp.where(chan == first + t * own, 1.0, 0.0).astype(BF)
        goal[t] = dot(pick, want, NT).astype(BF)

    def half_rows(h):
        return pl.ds(pl.multiple_of(h * hf, hf), hf)

    def tgt_copy(h, k, to_f, to):
        return rc(
            goal.at[to_f, half_rows(h)], tg.at[f, half_rows(h)],
            t_send.at[k, h], t_recv.at[f, h], to,
        )

    near_half, far_half = flip, 1 - flip
    crossing = (u + 1) // mid
    soon = flip + crossing * (1 - 2 * flip)
    later = 1 - soon
    tgt_copy(soon, 0, fp, p).start()
    tgt_copy(later, 0, fp, p).start()
    tg[f] = goal[f]

    ii = lax.broadcasted_iota(jnp.int32, (2 * half, 2 * half), 0)
    jj = lax.broadcasted_iota(jnp.int32, (2 * half, 2 * half), 1)
    spread_out = jnp.where(jj == 2 * (ii % half) + ii // half, 1.0, 0.0).astype(BF)
    gather_in = jnp.where(ii == 2 * (jj % half) + jj // half, 1.0, 0.0).astype(BF)

    def split_one(index, at, block_img):
        v = dot(spread_out, block_img, NN).astype(BF)
        x[index, at : at + half, :one] = v[:half]
        x[index, at : at + half, one:] = v[half:]

    def split_pair(index, i0, a, b):
        split_one(index, i0 * half, a)
        split_one(index, (i0 + 1) * half, b)
        va = dot(a, gather_in, TN).astype(BF)
        vb = dot(b, gather_in, TN).astype(BF)
        lanes = slice(i0 * half, (i0 + 2) * half)
        xt[index, :one, lanes] = jnp.concatenate([va[:, :half], vb[:, :half]], axis=1)
        xt[index, one:, lanes] = jnp.concatenate([va[:, half:], vb[:, half:]], axis=1)

    def split_row(t, row):
        for i0 in range(0, imgs, 2):
            split_pair(1 + 2 * t + row, i0, raw[t, i0, row], raw[t, i0 + 1, row])

    def img_step(j):
        img_wait(fq, j)
        fwd_copy(j).start()

    def rim_step():
        @pl.when(r > 0)
        def _():
            wait_in(rim_raw, r_recv)

            @pl.when(f == 3)
            def _():
                rim_to_q.start()

            @pl.when(f % 2 == 1)
            def _():
                rim_to_p.start()

    pass_on(1, 0)
    load_x.wait()
    for row in range(2):
        split_row(f, row)
    img_step(0)
    pass_on(1, 1)
    for j in range(len(order)):
        img_wait(fp, j)
    for row in range(2):
        split_row(fp, row)
    pass_on(1, 2)
    img_step(1)
    rim_step()

    @pl.when(r > 0)
    def _():
        for i0 in range(0, imgs, 2):
            split_pair(0, i0, rim_raw[i0], rim_raw[i0 + 1])

    @pl.when(r == 0)
    def _():
        x[0] = jnp.zeros((px, two), BF)
        xt[0] = jnp.zeros((two, px), BF)

    split_row(fq, 1)
    img_wait(fd, 0)
    img_wait(fd, 1)
    split_row(fd, 1)
    for h in range(2):
        wait_in(tg.at[fp, half_rows(h)], t_recv.at[fp, h])

    place = lax.broadcasted_iota(jnp.int32, (own, px), 1) % half

    def forward(b, tiles):
        rows = rows_of(b)
        for t in tiles:
            even = jnp.zeros((own, px), F32)
            odd = jnp.zeros((2 * own, px), F32)
            for kh in range(3):
                c = kh * three
                even += dot(w[rows, c + one : c + two], xt[2 * t + kh, :one], NN)
                both = jnp.concatenate([w[rows, c + two : c + three], w[rows, c : c + one]], axis=0)
                odd += dot(both, xt[2 * t + kh, one:], NN)
            left = jnp.where(place == 0, 0.0, pltpu.roll(odd[own:], 1, 1))
            out = even + odd[:own] + left
            grad = ((out - tg[t, rows].astype(F32)) * GRAD_SCALE).astype(BF)
            nxt = jnp.where(place == half - 1, 0.0, pltpu.roll(grad.astype(F32), px - 1, 1))
            gt[t, rows] = grad
            gts[t, rows] = nxt.astype(BF)

    def filter_terms(b):
        rows = rows_of(b)
        lhs = [gt[t, rows] for t in range(WIDE)]
        both = [jnp.concatenate([gts[t, rows], lhs[t]], axis=0) for t in range(WIDE)]
        sums = jnp.zeros((own, one), F32)
        for kh in range(3):
            c = kh * three
            even = dot(lhs[0], x[kh, :, :one], NN)
            odd = dot(both[0], x[kh, :, one:], NN)
            for t in range(1, WIDE):
                even += dot(lhs[t], x[2 * t + kh, :, :one], NN)
                odd += dot(both[t], x[2 * t + kh, :, one:], NN)
            g[rows, c : c + one] = odd[:own]
            g[rows, c + one : c + two] = even
            g[rows, c + two : c + three] = odd[own:]
            sums += even + odd[:own] + odd[own:]
        mean = jnp.sum(sums, axis=1, keepdims=True) * (1.0 / fan)
        for n in range(9):
            lanes = slice(n * one, (n + 1) * one)
            g[rows, lanes] = g[rows, lanes] - mean

    def g_copy(way, b, k, to):
        at = (way, rows_of(b), cols_of(k))
        return rc(part_out.at[at], part_in.at[at], g_send.at[way, b, k], g_recv.at[way, b, k], to)

    def g_wait(way, b, k):
        wait_in(part_in.at[way, rows_of(b), cols_of(k)], g_recv.at[way, b, k])

    def g_first(b, k):
        rows, cols = rows_of(b), cols_of(k)
        part_out[flip, rows, cols] = g[rows, cols].astype(BF)
        g_copy(flip, b, k, ahead_dev).start()

    def g_relay(way, b, k, to):
        rows, cols = rows_of(b), cols_of(k)
        g_wait(way, b, k)
        part_out[way, rows, cols] = (g[rows, cols] + part_in[way, rows, cols].astype(F32)).astype(BF)
        g_copy(way, b, k, to).start()

    def relay_lead(n, k):
        @pl.when(inside & (n > u))
        def _():
            g_relay(flip, block(n), k, ahead_dev)

    def relay_trail(n, k):
        @pl.when(inside & (n < u))
        def _():
            g_relay(1 - flip, block(n), k, behind_dev)

    first_b = block(u + 1)
    w_wait_end(first_b)

    def early(i, carry):
        forward(block(u + i), (f, fp))
        return carry

    lax.fori_loop(0, 2, early, 0)

    pass_on(2, 0)
    img_step(2)
    for k, (to_f, to) in ((1, (fq, q)), (2, (fd, d))):
        tgt_copy(soon, k, to_f, to).start()
    pass_on(2, 1)
    img_step(3)
    for k, (to_f, to) in ((1, (fq, q)), (2, (fd, d))):
        tgt_copy(later, k, to_f, to).start()
    split_row(fq, 0)
    img_wait(fd, 2)
    img_wait(fd, 3)
    split_row(fd, 0)
    pass_on(2, 2)
    for s in range(3, tall - 1):
        for k in range(PIECES):
            pass_on(s, k)
    for t in (fq, fd):
        wait_in(tg.at[t, half_rows(soon)], t_recv.at[t, soon])

    def turn(it, carry):
        i = jnp.where(it < 2, it + 1, jnp.where(it == 2, 0, it))
        n = nth(i)
        b = block(n)

        @pl.when((it == 1) | (it > 2))
        def _():
            w_wait_end(b)

        @pl.when(it == 1)
        def _():
            for t in (fq, fd):
                wait_in(tg.at[t, half_rows(later)], t_recv.at[t, later])

        @pl.when((it == 1) | (it > 2))
        def _():
            forward(b, (f, fp))

        forward(b, (fq, fd))
        filter_terms(b)

        @pl.when(at_end & (n == 1))
        def _():
            g_first(b, 0)

        @pl.when(at_end & (n > 1))
        def _():
            for k in range(PIECES):
                g_first(b, k)

        return carry

    lax.fori_loop(0, tall - 1, turn, 0)

    def turned(h):
        lanes = half_rows(h)
        for t in range(WIDE):
            gy[t, :, lanes] = gt[t, lanes].astype(F32).T.astype(BF)
            gys[t, :, lanes] = gts[t, lanes].astype(F32).T.astype(BF)

    gy[WIDE] = jnp.zeros((px, filters), BF)
    gys[WIDE] = jnp.zeros((px, filters), BF)
    turned(near_half)
    relay_lead(2, 0)
    last_n = tall - 1
    last_b = block(last_n)
    w_wait_end(last_b)
    forward(last_b, (f, fp))
    forward(last_b, (fq, fd))
    turned(far_half)
    relay_lead(2, 1)

    def taps(t, kh):
        c = kh * three
        even = dot(gy[t], w[:, c + one : c + two], NN)
        odd = dot(gy[t], w[:, c + two : c + three], NN)
        odd += dot(gys[t], w[:, c : c + one], NN)
        return even, odd

    def tile_row(t, row):
        if row == 0:
            return taps(t, 1)
        even, odd = taps(t, 2)
        more_even, more_odd = taps(t + 1, 0)
        return even + more_even, odd + more_odd

    halves = (slice(0, one), slice(one, two))
    rim_pc = rc(rim_s, rim_p, e_send, e_recv.at[0], p)
    rim_qc = rc(rim_s, rim_q, e_send, e_recv.at[1], q)
    rim_zc = rc(rim_s, rim_z, e_send, e_recv.at[2], above)

    def p_copy(k, row):
        at = (k, row)
        return rc(to_p.at[at], from_p.at[at], d_send.at[at], d_recv.at[at], p)

    def q_copy(row):
        return rc(to_q.at[row], from_q.at[row], d_send.at[2, row], d_recv.at[2, row], q)

    def for_p(k, t):
        for row in range(2):
            for part, lanes in zip(tile_row(t, row), halves):
                to_p[k, row, :, lanes] = part.astype(BF)
            p_copy(k, row).start()

    for_p(1, fd)
    relay_lead(2, 2)
    for row in range(2):
        sums = tile_row(fq, row)
        wait_in(from_p.at[1, row], d_recv.at[1, row])
        for part, lanes in zip(sums, halves):
            to_q[row, :, lanes] = (part + from_p[1, row, :, lanes].astype(F32)).astype(BF)
        q_copy(row).start()

    filter_terms(last_b)

    @pl.when(at_end)
    def _():
        for k in range(PIECES):
            g_first(last_b, k)
        for k in range(1, PIECES):
            g_first(first_b, k)

    @pl.when(r > 0)
    def _():
        edge = taps(0, 0)
        for part, lanes in zip(edge, halves):
            acc[0, :, lanes] = part

        @pl.when(f % 2 == 0)
        def _():
            rim_s[...] = acc[0].astype(BF)
            rim_pc.start()

        @pl.when(f == 1)
        def _():
            wait_in(rim_p, e_recv.at[0])
            rim_s[...] = (acc[0] + rim_p[...].astype(F32)).astype(BF)
            rim_qc.start()

        @pl.when(f == 3)
        def _():
            wait_in(rim_p, e_recv.at[0])
            acc[0] += rim_p[...].astype(F32)

    for_p(0, fp)

    def rim_last():
        @pl.when((r > 0) & (f == 3))
        def _():
            wait_in(rim_q, e_recv.at[1])
            rim_s[...] = (acc[0] + rim_q[...].astype(F32)).astype(BF)
            rim_zc.start()

    def relays(t, carry):
        relay_lead(t, 0)
        relay_lead(t, 1)
        relay_trail(tall - 1 - t, 0)
        relay_lead(t, 2)
        relay_trail(tall - 1 - t, 1)
        relay_trail(tall - 1 - t, 2)
        return carry

    lax.fori_loop(3, tall, relays, 0)
    rim_last()

    for row in range(2):
        for part, lanes in zip(tile_row(f, row), halves):
            acc[row, :, lanes] = part
    for row in range(2):
        wait_in(from_p.at[0, row], d_recv.at[0, row])
        wait_in(from_q.at[row], d_recv.at[2, row])
        if row == 1:
            @pl.when((r < tall - 1) & (f == 3))
            def _():
                wait_in(rim_z, e_recv.at[2])
                acc[1] += rim_z[...].astype(F32)

        total = (acc[row] + from_p[0, row].astype(F32) + from_q[row].astype(F32)).astype(BF)
        for i in range(imgs):
            mine = total[i * half : (i + 1) * half]
            stacked = jnp.concatenate([mine[:, :one], mine[:, one:]], axis=0)
            dout[i, row] = dot(gather_in, stacked, NN).astype(BF)

    mine = rows_of(r)

    @pl.when(r > 0)
    def _():
        for k in range(PIECES):
            g_wait(0, r, k)
        g[mine] += part_in[0, mine].astype(F32)

    @pl.when(r < tall - 1)
    def _():
        for k in range(PIECES):
            g_wait(1, r, k)
        g[mine] += part_in[1, mine].astype(F32)

    centre = stat[0][:, :1]
    inv = stat[1][:, :1]
    s1 = jnp.zeros((own, cin), F32)
    s2 = jnp.zeros((own, cin), F32)
    for n in range(9):
        hat = (wraw[n].astype(F32) - centre) * inv
        piece = g[mine, n * cin : (n + 1) * cin]
        s1 += piece
        s2 += piece * hat
    m1 = jnp.sum(s1, axis=1, keepdims=True) * (1.0 / fan)
    m2 = jnp.sum(s2, axis=1, keepdims=True) * (1.0 / fan)
    for n in range(9):
        hat = (wraw[n].astype(F32) - centre) * inv
        piece = g[mine, n * cin : (n + 1) * cin]
        gout[n] = (piece - m1 - hat * m2) * inv

    for j in range(len(order)):
        img_copy(j, 0, p).wait_send()
        img_copy(j, 1, q).wait_send()
        fwd_copy(j).wait_send()
    for h in range(2):
        tgt_copy(h, 0, fp, p).wait_send()
        tgt_copy(h, 1, fq, q).wait_send()
        tgt_copy(h, 2, fd, d).wait_send()
    for row in range(2):
        p_copy(0, row).wait_send()
        p_copy(1, row).wait_send()
        q_copy(row).wait_send()

    @pl.when((f == 3) & (r < tall - 1))
    def _():
        rim_in.wait_send()

    @pl.when((r > 0) & (f == 3))
    def _():
        rim_to_q.wait_send()

    @pl.when((r > 0) & (f % 2 == 1))
    def _():
        rim_to_p.wait_send()

    @pl.when(r > 0)
    def _():
        rim_pc.wait_send()

    def drain(b, carry):
        for k in range(PIECES):
            @pl.when((r < tall - 1) & (b <= r))
            def _():
                w_copy(b, k, 0).wait_send()

            @pl.when((r > 0) & (b >= r))
            def _():
                w_copy(b, k, 1).wait_send()

            @pl.when(b > r)
            def _():
                g_copy(0, b, k, p).wait_send()

            @pl.when(b < r)
            def _():
                g_copy(1, b, k, p).wait_send()

        return carry

    lax.fori_loop(0, tall, drain, 0)


def shards(images, target, raw_filters):
    imgs, two_rows, in_cols, cin = images.shape
    half = in_cols // 2
    own = raw_filters.shape[0]
    tall = lax.axis_size("space") // WIDE
    fan = 9 * cin
    px = imgs * half
    filters = tall * own
    wide = target.shape[3]
    vm = pltpu.VMEM
    dma = pltpu.SemaphoreType.DMA
    row = (px, 2 * cin)
    scratch = [
        vm((WIDE,) + images.shape, BF), vm((imgs, in_cols, cin), BF), vm((imgs, half, wide), BF),
        vm((9, own, cin), BF), vm((2, own, 128), F32),
        vm((2 * WIDE + 1,) + row, BF), vm((2 * WIDE + 1, 2 * cin, px), BF), vm((filters, fan), BF),
        vm((WIDE, filters, px), BF), vm((WIDE, filters, px), BF),
        vm((WIDE + 1, px, filters), BF), vm((WIDE + 1, px, filters), BF),
        vm((WIDE, filters, px), BF), vm((WIDE, filters, px), BF), vm((filters, fan), F32),
        vm((2, filters, fan), BF), vm((2, filters, fan), BF),
        vm((2, 2) + row, BF), vm((2, 2) + row, BF), vm((2,) + row, BF), vm((2,) + row, BF),
        vm((2,) + row, F32), vm(row, BF), vm(row, BF), vm(row, BF), vm(row, BF),
        dma((3,)), dma((WIDE, 4)), dma((3, 4)), dma((tall, PIECES)), dma((2, tall, PIECES)),
        dma((WIDE, 2)), dma((3, 2)), dma, dma((3,)),
        dma((2, tall, PIECES)), dma((2, tall, PIECES)), dma((3, 2)), dma((3, 2)), dma((3,)), dma,
    ]
    input_grads, by_tap = pl.pallas_call(
        functools.partial(kernel, tall, own, half, cin),
        out_shape=(
            jax.ShapeDtypeStruct(images.shape, BF),
            jax.ShapeDtypeStruct((9, own, cin), F32),
        ),
        in_specs=[pl.BlockSpec(memory_space=pl.ANY)] * 3,
        out_specs=[pl.BlockSpec(memory_space=pltpu.VMEM)] * 2,
        scratch_shapes=scratch,
        compiler_params=pltpu.CompilerParams(
            collective_id=0, has_side_effects=True, vmem_limit_bytes=60 * 1024 * 1024
        ),
        name="tiles",
    )(
        images,
        target.reshape(imgs, half, wide),
        raw_filters.transpose(1, 2, 0, 3).reshape(9, own, cin),
    )
    filter_grads = by_tap.reshape(3, 3, own, cin).transpose(2, 0, 1, 3)
    return (input_grads, filter_grads)


def solution(mesh):
    return jax.shard_map(
        shards,
        mesh=mesh,
        in_specs=(
            P("parts", "space", None, None),
            P("parts", "space", None, None),
            P(("parts", "space"), None, None, None),
        ),
        out_specs=(P("parts", "space", None, None), P(("parts", "space"), None, None, None)),
        check_vma=False,
    )
```

```python
import functools

import jax
import jax.numpy as jnp
from jax import lax
from jax.experimental import pallas as pl
from jax.experimental.pallas import tpu as pltpu
from jax.sharding import PartitionSpec as P

EPS = 1e-05
GRAD_SCALE = 0.015625
WIDE = 4
PIECES = 3
STRIPS = 6
START = 2
F32 = jnp.float32
BF = jnp.bfloat16
NT = (((1,), (1,)), ((), ()))
NN = (((1,), (0,)), ((), ()))
TN = (((0,), (0,)), ((), ()))
MESH = pl.DeviceIdType.MESH


def dot(a, b, dims):
    return lax.dot_general(a, b, dims, preferred_element_type=F32)


def kernel(
    tall, own, half, cin,
    images, target, filters_in, dout_hbm, gout_hbm,
    dout, gout, raw, rim_raw, goal_raw, wraw, stat,
    x, xt, w, goal, tg, gy, gys, gt, gts, g, part_in, part_out,
    to_p, from_p, to_q, from_q, acc, rim_x, rim_p, rim_s, rim_z,
    l_sem, o_sem, i_recv, i_send, w_recv, w_send, t_recv, t_send, r_recv, r_send,
    g_recv, g_send, d_recv, d_send, e_recv, e_send,
):
    me = lax.axis_index("space")
    r, f = me // WIDE, me % WIDE
    base = r * WIDE
    fp = f + 1 - 2 * (f % 2)
    fq = f + 2 - 4 * (f // 2)
    fd = fp + 2 - 4 * (fp // 2)
    p, q, d = base + fp, base + fq, base + fd
    above, below = me - WIDE, me + WIDE
    imgs = images.shape[0]
    px = imgs * half
    two, one = 2 * cin, cin
    three = 3 * cin
    filters = tall * own
    fan = 9 * cin
    mid = tall // 2
    hf = filters // 2
    flip = r // mid
    u = r + flip * (tall - 1 - 2 * r)
    ahead_dev = me + WIDE - 2 * WIDE * flip
    behind_dev = me - WIDE + 2 * WIDE * flip
    at_end = u == 0
    inside = u > 0

    def rc(src, dst, ssem, rsem, to):
        return pltpu.make_async_remote_copy(
            src_ref=src, dst_ref=dst, send_sem=ssem, recv_sem=rsem,
            device_id={"space": to}, device_id_type=MESH,
        )

    def wait_in(dst, rsem):
        rc(dst, dst, rsem, rsem, p).wait_recv()

    def rows_of(b):
        return pl.ds(pl.multiple_of(b * own, own), own)

    wide_cols = fan // PIECES

    def cols_of(k):
        return slice(k * wide_cols, (k + 1) * wide_cols)

    strip_cols = fan // STRIPS

    def strip_of(k):
        return slice(k * strip_cols, (k + 1) * strip_cols)

    def block(n):
        return n + flip * (tall - 1 - 2 * n)

    def nth(i):
        near = jnp.where(i % 2 == 1, u + (i + 1) // 2, u - i // 2)
        return jnp.where(i > 2 * u, i, near)

    bar = pltpu.get_barrier_semaphore()

    def greet(to):
        pl.semaphore_signal(bar, inc=1, device_id={"space": to}, device_id_type=MESH)

    for to in (p, q, d):
        greet(to)

    @pl.when(r > 0)
    def _():
        greet(above)

    @pl.when(r < tall - 1)
    def _():
        greet(below)

    load_w = pltpu.make_async_copy(filters_in, wraw, l_sem.at[0])
    load_x = pltpu.make_async_copy(images, raw.at[f], l_sem.at[1])
    load_t = pltpu.make_async_copy(target, goal_raw, l_sem.at[2])
    load_w.start()
    load_x.start()
    load_t.start()

    @pl.when((r < tall - 1) & (f % 2 == 1))
    def _():
        greet(below - 1)

    more = (r > 0) & (f % 2 == 0)
    fewer = jnp.logical_not(more)

    @pl.when(inside & more)
    def _():
        pl.semaphore_wait(bar, 6)

    @pl.when((inside & fewer) | (at_end & more))
    def _():
        pl.semaphore_wait(bar, 5)

    @pl.when(at_end & fewer)
    def _():
        pl.semaphore_wait(bar, 4)

    pairs = 2
    per = imgs // pairs
    order = [(row, h) for row in (1, 0) for h in range(pairs)]

    def piece_of(ref, j):
        row, h = order[j]
        return ref.at[slice(h * per, (h + 1) * per), row]

    def img_copy(j, k, to):
        return rc(piece_of(images, j), piece_of(raw.at[f], j), i_send.at[k, j], i_recv.at[f, j], to)

    def fwd_copy(j):
        slot = piece_of(raw.at[fq], j)
        return rc(slot, slot, i_send.at[2, j], i_recv.at[fq, j], p)

    def img_wait(t, j):
        wait_in(piece_of(raw.at[t], j), i_recv.at[t, j])

    rim_in = rc(images.at[:, 1], rim_raw, r_send.at[0], r_recv, below)
    rim_via = rc(raw.at[fq, :, 1], rim_raw, r_send.at[0], r_recv, below)
    rim_to_p = rc(rim_raw, rim_raw, r_send.at[1], r_recv, p)

    for j in range(len(order)):
        img_copy(j, 1, q).start()

    @pl.when((f == 3) & (r < tall - 1))
    def _():
        rim_in.start()

    def w_copy(b, k, way):
        slot = w.at[rows_of(b), cols_of(k)]
        to = below if way == 0 else above
        return rc(slot, slot, w_send.at[way, b, k], w_recv.at[b, k], to)

    load_w.wait()
    centre = wraw[0].astype(F32)
    for k in range(1, 9):
        centre += wraw[k].astype(F32)
    centre = jnp.sum(centre, axis=1, keepdims=True) * (1.0 / fan)
    spread = jnp.zeros((own, cin), F32)
    for k in range(9):
        off = wraw[k].astype(F32) - centre
        spread += off * off
    spread = jnp.sqrt(jnp.sum(spread, axis=1, keepdims=True) * (1.0 / fan) + EPS)
    inv = 1.0 / spread
    stat[0] = jnp.broadcast_to(centre, (own, 128))
    stat[1] = jnp.broadcast_to(inv, (own, 128))
    taps_per = 9 // PIECES
    for k in range(PIECES):
        for n in range(k * taps_per, (k + 1) * taps_per):
            w[rows_of(r), n * cin : (n + 1) * cin] = ((wraw[n].astype(F32) - centre) * inv).astype(BF)

        @pl.when(r < tall - 1)
        def _():
            w_copy(r, k, 0).start()

        @pl.when(r > 0)
        def _():
            w_copy(r, k, 1).start()

    for j in range(len(order)):
        img_copy(j, 0, p).start()

    def pass_on(s, k):
        up, dn = r - s, r + s

        @pl.when(inside & (up >= 0))
        def _():
            wait_in(w.at[rows_of(up), cols_of(k)], w_recv.at[up, k])
            w_copy(up, k, 0).start()

        @pl.when(inside & (dn <= tall - 1))
        def _():
            wait_in(w.at[rows_of(dn), cols_of(k)], w_recv.at[dn, k])
            w_copy(dn, k, 1).start()

    def w_wait_end(b):
        @pl.when(at_end)
        def _():
            for k in range(PIECES):
                wait_in(w.at[rows_of(b), cols_of(k)], w_recv.at[b, k])

    load_t.wait()
    want = goal_raw[...].reshape(px, goal_raw.shape[2])
    wide = goal_raw.shape[2]
    line = lax.broadcasted_iota(jnp.int32, (filters, wide), 0)
    chan = lax.broadcasted_iota(jnp.int32, (filters, wide), 1)
    first = (line // own) * (own * WIDE) + line % own
    for t in range(WIDE):
        pick = jnp.where(chan == first + t * own, 1.0, 0.0).astype(BF)
        goal[t] = dot(pick, want, NT).astype(BF)

    def half_rows(h):
        return pl.ds(pl.multiple_of(h * hf, hf), hf)

    def tgt_copy(h, k, to_f, to):
        return rc(
            goal.at[to_f, half_rows(h)], tg.at[f, half_rows(h)],
            t_send.at[k, h], t_recv.at[f, h], to,
        )

    near_half, far_half = flip, 1 - flip
    crossing = (u + 1) // mid
    soon = flip + crossing * (1 - 2 * flip)
    later = 1 - soon
    tgt_copy(soon, 0, fp, p).start()
    tgt_copy(later, 0, fp, p).start()
    tg[f] = goal[f]

    ii = lax.broadcasted_iota(jnp.int32, (2 * half, 2 * half), 0)
    jj = lax.broadcasted_iota(jnp.int32, (2 * half, 2 * half), 1)
    spread_out = jnp.where(jj == 2 * (ii % half) + ii // half, 1.0, 0.0).astype(BF)
    gather_in = jnp.where(ii == 2 * (jj % half) + jj // half, 1.0, 0.0).astype(BF)

    def split_one(index, at, block_img):
        v = dot(spread_out, block_img, NN).astype(BF)
        x[index, at : at + half, :one] = v[:half]
        x[index, at : at + half, one:] = v[half:]

    def split_pair(index, i0, a, b):
        split_one(index, i0 * half, a)
        split_one(index, (i0 + 1) * half, b)
        va = dot(a, gather_in, TN).astype(BF)
        vb = dot(b, gather_in, TN).astype(BF)
        lanes = slice(i0 * half, (i0 + 2) * half)
        xt[index, :one, lanes] = jnp.concatenate([va[:, :half], vb[:, :half]], axis=1)
        xt[index, one:, lanes] = jnp.concatenate([va[:, half:], vb[:, half:]], axis=1)

    def split_row(t, row):
        for i0 in range(0, imgs, 2):
            split_pair(1 + 2 * t + row, i0, raw[t, i0, row], raw[t, i0 + 1, row])

    def img_step(j):
        img_wait(fq, j)
        fwd_copy(j).start()

    def rim_step():
        @pl.when(r > 0)
        def _():
            wait_in(rim_raw, r_recv)

            @pl.when(f % 2 == 1)
            def _():
                rim_to_p.start()

    pass_on(1, 0)
    load_x.wait()
    for row in range(2):
        split_row(f, row)
    img_step(0)
    pass_on(1, 1)
    for j in range(len(order)):
        img_wait(fp, j)
    for row in range(2):
        split_row(fp, row)
    pass_on(1, 2)
    img_step(1)

    @pl.when((f == 1) & (r < tall - 1))
    def _():
        rim_via.start()

    split_row(fq, 1)
    img_wait(fd, 0)
    img_wait(fd, 1)
    split_row(fd, 1)
    for h in range(2):
        wait_in(tg.at[fp, half_rows(h)], t_recv.at[fp, h])

    place = lax.broadcasted_iota(jnp.int32, (own, px), 1) % half

    def forward(b, tiles):
        rows = rows_of(b)
        for t in tiles:
            even = jnp.zeros((own, px), F32)
            odd = jnp.zeros((2 * own, px), F32)
            for kh in range(3):
                c = kh * three
                even += dot(w[rows, c + one : c + two], xt[2 * t + kh, :one], NN)
                both = jnp.concatenate([w[rows, c + two : c + three], w[rows, c : c + one]], axis=0)
                odd += dot(both, xt[2 * t + kh, one:], NN)
            left = jnp.where(place == 0, 0.0, pltpu.roll(odd[own:], 1, 1))
            out = even + odd[:own] + left
            grad = ((out - tg[t, rows].astype(F32)) * GRAD_SCALE).astype(BF)
            nxt = jnp.where(place == half - 1, 0.0, pltpu.roll(grad.astype(F32), px - 1, 1))
            gt[t, rows] = grad
            gts[t, rows] = nxt.astype(BF)

    def filter_terms(b):
        rows = rows_of(b)
        lhs = [gt[t, rows] for t in range(WIDE)]
        both = [jnp.concatenate([gts[t, rows], lhs[t]], axis=0) for t in range(WIDE)]
        sums = jnp.zeros((own, one), F32)
        for kh in range(3):
            c = kh * three
            even = dot(lhs[0], x[kh, :, :one], NN)
            odd = dot(both[0], x[kh, :, one:], NN)
            for t in range(1, WIDE):
                even += dot(lhs[t], x[2 * t + kh, :, :one], NN)
                odd += dot(both[t], x[2 * t + kh, :, one:], NN)
            g[rows, c : c + one] = odd[:own]
            g[rows, c + one : c + two] = even
            g[rows, c + two : c + three] = odd[own:]
            sums += even + odd[:own] + odd[own:]
        mean = jnp.sum(sums, axis=1, keepdims=True) * (1.0 / fan)
        for n in range(9):
            lanes = slice(n * one, (n + 1) * one)
            g[rows, lanes] = g[rows, lanes] - mean

    def g_copy(way, b, k, to):
        at = (way, rows_of(b), strip_of(k))
        return rc(part_out.at[at], part_in.at[at], g_send.at[way, b, k], g_recv.at[way, b, k], to)

    def g_wait(way, b, k):
        wait_in(part_in.at[way, rows_of(b), strip_of(k)], g_recv.at[way, b, k])

    def g_first(b, k):
        rows, cols = rows_of(b), strip_of(k)
        part_out[flip, rows, cols] = g[rows, cols].astype(BF)
        g_copy(flip, b, k, ahead_dev).start()

    def g_relay(way, b, k, to):
        rows, cols = rows_of(b), strip_of(k)
        g_wait(way, b, k)
        part_out[way, rows, cols] = (g[rows, cols] + part_in[way, rows, cols].astype(F32)).astype(BF)
        g_copy(way, b, k, to).start()

    def relay_lead(n, k):
        @pl.when(inside & (n > u))
        def _():
            g_relay(flip, block(n), k, ahead_dev)

    def relay_trail(n, k):
        @pl.when(inside & (n < u))
        def _():
            g_relay(1 - flip, block(n), k, behind_dev)

    pass_on(2, 0)
    img_step(2)
    for k, (to_f, to) in ((1, (fq, q)), (2, (fd, d))):
        tgt_copy(soon, k, to_f, to).start()
    rim_step()

    @pl.when(r > 0)
    def _():
        for i0 in range(0, imgs, 2):
            split_pair(0, i0, rim_raw[i0], rim_raw[i0 + 1])

    @pl.when(r == 0)
    def _():
        x[0] = jnp.zeros((px, two), BF)
        xt[0] = jnp.zeros((two, px), BF)

    first_b = block(u + 1)
    w_wait_end(first_b)

    def early(i, carry):
        forward(block(u + i), (f, fp))
        return carry

    lax.fori_loop(0, 2, early, 0)

    pass_on(2, 1)
    img_step(3)
    for k, (to_f, to) in ((1, (fq, q)), (2, (fd, d))):
        tgt_copy(later, k, to_f, to).start()
    split_row(fq, 0)
    img_wait(fd, 2)
    img_wait(fd, 3)
    split_row(fd, 0)
    pass_on(2, 2)
    for s in range(3, tall - 1):
        for k in range(PIECES):
            pass_on(s, k)
    for t in (fq, fd):
        wait_in(tg.at[t, half_rows(soon)], t_recv.at[t, soon])

    def turn(it, carry):
        i = jnp.where(it < 2, it + 1, jnp.where(it == 2, 0, it))
        n = nth(i)
        b = block(n)

        @pl.when((it == 1) | (it > 2))
        def _():
            w_wait_end(b)

        @pl.when(it == 1)
        def _():
            for t in (fq, fd):
                wait_in(tg.at[t, half_rows(later)], t_recv.at[t, later])

        @pl.when((it == 1) | (it > 2))
        def _():
            forward(b, (f, fp))

        forward(b, (fq, fd))
        filter_terms(b)

        @pl.when(at_end & (n == 1))
        def _():
            for k in range(START):
                g_first(b, k)

        @pl.when(at_end & (n > 1))
        def _():
            for k in range(STRIPS):
                g_first(b, k)

        return carry

    lax.fori_loop(0, tall - 1, turn, 0)

    def turned(h):
        lanes = half_rows(h)
        for t in range(WIDE):
            gy[t, :, lanes] = gt[t, lanes].astype(F32).T.astype(BF)
            gys[t, :, lanes] = gts[t, lanes].astype(F32).T.astype(BF)

    gy[WIDE] = jnp.zeros((px, filters), BF)
    gys[WIDE] = jnp.zeros((px, filters), BF)
    turned(near_half)
    relay_lead(2, 0)
    relay_lead(2, 1)
    last_n = tall - 1
    last_b = block(last_n)
    w_wait_end(last_b)
    forward(last_b, (f, fp))
    forward(last_b, (fq, fd))
    turned(far_half)
    relay_lead(2, 2)
    relay_lead(2, 3)

    def taps(t, kh):
        c = kh * three
        even = dot(gy[t], w[:, c + one : c + two], NN)
        odd = dot(gy[t], w[:, c + two : c + three], NN)
        odd += dot(gys[t], w[:, c : c + one], NN)
        return even, odd

    def tile_row(t, row):
        if row == 0:
            return taps(t, 1)
        even, odd = taps(t, 2)
        more_even, more_odd = taps(t + 1, 0)
        return even + more_even, odd + more_odd

    halves = (slice(0, one), slice(one, two))
    c = f % 2
    half_px = px // 2
    keep = pl.ds(pl.multiple_of(c * half_px, half_px), half_px)
    give = pl.ds(pl.multiple_of((1 - c) * half_px, half_px), half_px)
    rim_pc = rc(rim_x.at[give], rim_p, e_send.at[0], e_recv.at[0], p)
    rim_zc = rc(rim_s, rim_z.at[keep], e_send.at[1], e_recv.at[1 + c], above + 1 - c)

    def rim_zwait():
        for n in range(2):
            part = slice(n * half_px, (n + 1) * half_px)
            wait_in(rim_z.at[part], e_recv.at[1 + n])

    def p_copy(k, row):
        at = (k, row)
        return rc(to_p.at[at], from_p.at[at], d_send.at[at], d_recv.at[at], p)

    def q_copy(row):
        return rc(to_q.at[row], from_q.at[row], d_send.at[2, row], d_recv.at[2, row], q)

    def for_p(k, t):
        for row in range(2):
            for part, lanes in zip(tile_row(t, row), halves):
                to_p[k, row, :, lanes] = part.astype(BF)
            p_copy(k, row).start()

    def for_q(row):
        sums = tile_row(fq, row)
        wait_in(from_p.at[1, row], d_recv.at[1, row])
        for part, lanes in zip(sums, halves):
            acc[row, :, lanes] = part + from_p[1, row, :, lanes].astype(F32)

    @pl.when(r > 0)
    def _():
        edge = taps(0, 0)
        for part, lanes in zip(edge, halves):
            rim_x[:, lanes] = part.astype(BF)
        rim_pc.start()

    for_p(1, fd)
    relay_lead(2, 4)
    relay_lead(2, 5)

    @pl.when(r > 0)
    def _():
        wait_in(rim_p, e_recv.at[0])
        rim_s[...] = (rim_x[keep].astype(F32) + rim_p[...].astype(F32)).astype(BF)
        rim_zc.start()

    for_q(0)
    to_q[0] = acc[0].astype(BF)
    q_copy(0).start()
    filter_terms(last_b)

    @pl.when(at_end)
    def _():
        for k in range(STRIPS):
            g_first(last_b, k)
        for k in range(START, STRIPS):
            g_first(first_b, k)

    for_q(1)
    for_p(0, fp)
    relay_lead(3, 0)
    relay_lead(3, 1)

    @pl.when((f == 1) & (r < tall - 1))
    def _():
        rim_zwait()
        acc[1] += rim_z[...].astype(F32)

    to_q[1] = acc[1].astype(BF)
    q_copy(1).start()
    relay_lead(3, 2)
    relay_trail(tall - 4, 0)
    for k in range(3, STRIPS):
        relay_lead(3, k)
        relay_trail(tall - 4, k - 2)
    relay_trail(tall - 4, STRIPS - 2)
    relay_trail(tall - 4, STRIPS - 1)

    def relays(t, carry):
        for k in range(STRIPS):
            relay_lead(t, k)
            relay_trail(tall - 1 - t, k)
        return carry

    if tall > 4:
        lax.fori_loop(4, tall, relays, 0)

    def out_row(row):
        return pltpu.make_async_copy(dout.at[:, row], dout_hbm.at[:, row], o_sem.at[row])

    for row in range(2):
        for part, lanes in zip(tile_row(f, row), halves):
            acc[row, :, lanes] = part
        wait_in(from_p.at[0, row], d_recv.at[0, row])
        acc[row] += from_p[0, row].astype(F32)

    @pl.when((r < tall - 1) & (f == 3))
    def _():
        rim_zwait()
        acc[1] += rim_z[...].astype(F32)

    def finish_row(row):
        wait_in(from_q.at[row], d_recv.at[2, row])
        total = (acc[row] + from_q[row].astype(F32)).astype(BF)
        for i in range(imgs):
            mine = total[i * half : (i + 1) * half]
            stacked = jnp.concatenate([mine[:, :one], mine[:, one:]], axis=0)
            dout[i, row] = dot(gather_in, stacked, NN).astype(BF)
        out_row(row).start()

    finish_row(0)

    mine = rows_of(r)

    @pl.when(r > 0)
    def _():
        for k in range(STRIPS):
            g_wait(0, r, k)
        g[mine] += part_in[0, mine].astype(F32)

    @pl.when(r < tall - 1)
    def _():
        for k in range(STRIPS):
            g_wait(1, r, k)
        g[mine] += part_in[1, mine].astype(F32)

    centre = stat[0][:, :1]
    inv = stat[1][:, :1]
    s1 = jnp.zeros((own, cin), F32)
    s2 = jnp.zeros((own, cin), F32)
    for n in range(9):
        hat = (wraw[n].astype(F32) - centre) * inv
        piece = g[mine, n * cin : (n + 1) * cin]
        s1 += piece
        s2 += piece * hat
    m1 = jnp.sum(s1, axis=1, keepdims=True) * (1.0 / fan)
    m2 = jnp.sum(s2, axis=1, keepdims=True) * (1.0 / fan)
    for n in range(9):
        hat = (wraw[n].astype(F32) - centre) * inv
        piece = g[mine, n * cin : (n + 1) * cin]
        gout[n] = (piece - m1 - hat * m2) * inv
    out_g = pltpu.make_async_copy(gout, gout_hbm, o_sem.at[2])
    out_g.start()
    finish_row(1)

    for j in range(len(order)):
        img_copy(j, 0, p).wait_send()
        img_copy(j, 1, q).wait_send()
        fwd_copy(j).wait_send()
    for h in range(2):
        tgt_copy(h, 0, fp, p).wait_send()
        tgt_copy(h, 1, fq, q).wait_send()
        tgt_copy(h, 2, fd, d).wait_send()
    for row in range(2):
        p_copy(0, row).wait_send()
        p_copy(1, row).wait_send()
        q_copy(row).wait_send()

    @pl.when((f % 2 == 1) & (r < tall - 1))
    def _():
        rim_in.wait_send()

    @pl.when((r > 0) & (f % 2 == 1))
    def _():
        rim_to_p.wait_send()

    @pl.when(r > 0)
    def _():
        rim_pc.wait_send()
        rim_zc.wait_send()

    def drain(b, carry):
        for k in range(PIECES):
            @pl.when((r < tall - 1) & (b <= r))
            def _():
                w_copy(b, k, 0).wait_send()

            @pl.when((r > 0) & (b >= r))
            def _():
                w_copy(b, k, 1).wait_send()

        for k in range(STRIPS):
            @pl.when(b > r)
            def _():
                g_copy(0, b, k, p).wait_send()

            @pl.when(b < r)
            def _():
                g_copy(1, b, k, p).wait_send()

        return carry

    lax.fori_loop(0, tall, drain, 0)
    out_g.wait()
    for row in range(2):
        out_row(row).wait()


def shards(images, target, raw_filters):
    imgs, two_rows, in_cols, cin = images.shape
    half = in_cols // 2
    own = raw_filters.shape[0]
    tall = lax.axis_size("space") // WIDE
    fan = 9 * cin
    px = imgs * half
    filters = tall * own
    wide = target.shape[3]
    vm = pltpu.VMEM
    dma = pltpu.SemaphoreType.DMA
    row = (px, 2 * cin)
    scratch = [
        vm(images.shape, BF), vm((9, own, cin), F32),
        vm((WIDE,) + images.shape, BF), vm((imgs, in_cols, cin), BF), vm((imgs, half, wide), BF),
        vm((9, own, cin), BF), vm((2, own, 128), F32),
        vm((2 * WIDE + 1,) + row, BF), vm((2 * WIDE + 1, 2 * cin, px), BF), vm((filters, fan), BF),
        vm((WIDE, filters, px), BF), vm((WIDE, filters, px), BF),
        vm((WIDE + 1, px, filters), BF), vm((WIDE + 1, px, filters), BF),
        vm((WIDE, filters, px), BF), vm((WIDE, filters, px), BF), vm((filters, fan), F32),
        vm((2, filters, fan), BF), vm((2, filters, fan), BF),
        vm((2, 2) + row, BF), vm((2, 2) + row, BF), vm((2,) + row, BF), vm((2,) + row, BF),
        vm((2,) + row, F32),
        vm(row, BF), vm((px // 2, 2 * cin), BF), vm((px // 2, 2 * cin), BF), vm(row, BF),
        dma((3,)), dma((3,)), dma((WIDE, 4)), dma((3, 4)), dma((tall, PIECES)), dma((2, tall, PIECES)),
        dma((WIDE, 2)), dma((3, 2)), dma, dma((2,)),
        dma((2, tall, STRIPS)), dma((2, tall, STRIPS)), dma((3, 2)), dma((3, 2)), dma((3,)), dma((2,)),
    ]
    input_grads, by_tap = pl.pallas_call(
        functools.partial(kernel, tall, own, half, cin),
        out_shape=(
            jax.ShapeDtypeStruct(images.shape, BF),
            jax.ShapeDtypeStruct((9, own, cin), F32),
        ),
        in_specs=[pl.BlockSpec(memory_space=pl.ANY)] * 3,
        out_specs=[pl.BlockSpec(memory_space=pl.ANY)] * 2,
        scratch_shapes=scratch,
        compiler_params=pltpu.CompilerParams(
            collective_id=0, has_side_effects=True, vmem_limit_bytes=60 * 1024 * 1024
        ),
        name="tiles",
    )(
        images,
        target.reshape(imgs, half, wide),
        raw_filters.transpose(1, 2, 0, 3).reshape(9, own, cin),
    )
    filter_grads = by_tap.reshape(3, 3, own, cin).transpose(2, 0, 1, 3)
    return (input_grads, filter_grads)


def solution(mesh):
    return jax.shard_map(
        shards,
        mesh=mesh,
        in_specs=(
            P("parts", "space", None, None),
            P("parts", "space", None, None),
            P(("parts", "space"), None, None, None),
        ),
        out_specs=(P("parts", "space", None, None), P(("parts", "space"), None, None, None)),
        check_vma=False,
    )
```

```python
import functools

import jax
import jax.numpy as jnp
from jax import lax
from jax.experimental import pallas as pl
from jax.experimental.pallas import tpu as pltpu
from jax.sharding import PartitionSpec as P

EPS = 1e-05
GRAD_SCALE = 0.015625
WIDE = 4
PIECES = 3
STRIPS = 6
START = 3
F32 = jnp.float32
BF = jnp.bfloat16
NT = (((1,), (1,)), ((), ()))
NN = (((1,), (0,)), ((), ()))
TN = (((0,), (0,)), ((), ()))
MESH = pl.DeviceIdType.MESH


def dot(a, b, dims):
    return lax.dot_general(a, b, dims, preferred_element_type=F32)


def kernel(
    tall, own, half, cin,
    images, target, filters_in, dout_hbm, gout_hbm,
    dout, gout, raw, rim_raw, goal_raw, wraw, stat,
    x, xt, w, goal, tg, gy, gys, gt, gts, g, part_in, part_out,
    to_p, from_p, to_q, from_q, acc, rim_x, rim_p, rim_s, rim_z,
    l_sem, o_sem, i_recv, i_send, w_recv, w_send, t_recv, t_send, r_recv, r_send,
    g_recv, g_send, d_recv, d_send, e_recv, e_send,
):
    me = lax.axis_index("space")
    r, f = me // WIDE, me % WIDE
    base = r * WIDE
    fp = f + 1 - 2 * (f % 2)
    fq = f + 2 - 4 * (f // 2)
    fd = fp + 2 - 4 * (fp // 2)
    p, q, d = base + fp, base + fq, base + fd
    above, below = me - WIDE, me + WIDE
    imgs = images.shape[0]
    px = imgs * half
    two, one = 2 * cin, cin
    three = 3 * cin
    filters = tall * own
    fan = 9 * cin
    mid = tall // 2
    hf = filters // 2
    flip = r // mid
    u = r + flip * (tall - 1 - 2 * r)
    ahead_dev = me + WIDE - 2 * WIDE * flip
    behind_dev = me - WIDE + 2 * WIDE * flip
    at_end = u == 0
    inside = u > 0

    def rc(src, dst, ssem, rsem, to):
        return pltpu.make_async_remote_copy(
            src_ref=src, dst_ref=dst, send_sem=ssem, recv_sem=rsem,
            device_id={"space": to}, device_id_type=MESH,
        )

    def wait_in(dst, rsem):
        rc(dst, dst, rsem, rsem, p).wait_recv()

    def rows_of(b):
        return pl.ds(pl.multiple_of(b * own, own), own)

    wide_cols = fan // PIECES

    def cols_of(k):
        return slice(k * wide_cols, (k + 1) * wide_cols)

    strip_cols = fan // STRIPS

    def strip_of(k):
        return slice(k * strip_cols, (k + 1) * strip_cols)

    def block(n):
        return n + flip * (tall - 1 - 2 * n)

    def nth(i):
        near = jnp.where(i % 2 == 1, u + (i + 1) // 2, u - i // 2)
        return jnp.where(i > 2 * u, i, near)

    bar = pltpu.get_barrier_semaphore()

    def greet(to):
        pl.semaphore_signal(bar, inc=1, device_id={"space": to}, device_id_type=MESH)

    for to in (p, q, d):
        greet(to)

    @pl.when(r > 0)
    def _():
        greet(above)

    @pl.when(r < tall - 1)
    def _():
        greet(below)

    load_w = pltpu.make_async_copy(filters_in, wraw, l_sem.at[0])
    load_x = pltpu.make_async_copy(images, raw.at[f], l_sem.at[1])
    load_t = pltpu.make_async_copy(target, goal_raw, l_sem.at[2])
    load_w.start()
    load_x.start()
    load_t.start()

    @pl.when((r < tall - 1) & (f % 2 == 1))
    def _():
        greet(below - 1)

    more = (r > 0) & (f % 2 == 0)
    fewer = jnp.logical_not(more)

    @pl.when(inside & more)
    def _():
        pl.semaphore_wait(bar, 6)

    @pl.when((inside & fewer) | (at_end & more))
    def _():
        pl.semaphore_wait(bar, 5)

    @pl.when(at_end & fewer)
    def _():
        pl.semaphore_wait(bar, 4)

    pairs = 2
    per = imgs // pairs
    order = [(row, h) for row in (1, 0) for h in range(pairs)]

    def piece_of(ref, j):
        row, h = order[j]
        return ref.at[slice(h * per, (h + 1) * per), row]

    def img_copy(j, k, to):
        return rc(piece_of(images, j), piece_of(raw.at[f], j), i_send.at[k, j], i_recv.at[f, j], to)

    def fwd_copy(j):
        slot = piece_of(raw.at[fq], j)
        return rc(slot, slot, i_send.at[2, j], i_recv.at[fq, j], p)

    def img_wait(t, j):
        wait_in(piece_of(raw.at[t], j), i_recv.at[t, j])

    c = f % 2
    share = rim_raw.at[pl.ds(c * per, per)]
    other = rim_raw.at[pl.ds((1 - c) * per, per)]
    rim_in = rc(images.at[pl.ds(c * per, per), 1], share, r_send.at[0], r_recv.at[0], below)
    rim_via = rc(raw.at[WIDE - 1, pl.ds(c * per, per), 1], share, r_send.at[0], r_recv.at[0], below)
    rim_to_p = rc(share, share, r_send.at[1], r_recv.at[1], p)

    for j in range(len(order)):
        img_copy(j, 1, q).start()

    @pl.when((f == 3) & (r < tall - 1))
    def _():
        rim_in.start()

    def w_copy(b, k, way):
        slot = w.at[rows_of(b), cols_of(k)]
        to = below if way == 0 else above
        return rc(slot, slot, w_send.at[way, b, k], w_recv.at[b, k], to)

    load_w.wait()
    centre = wraw[0].astype(F32)
    for k in range(1, 9):
        centre += wraw[k].astype(F32)
    centre = jnp.sum(centre, axis=1, keepdims=True) * (1.0 / fan)
    spread = jnp.zeros((own, cin), F32)
    for k in range(9):
        off = wraw[k].astype(F32) - centre
        spread += off * off
    spread = jnp.sqrt(jnp.sum(spread, axis=1, keepdims=True) * (1.0 / fan) + EPS)
    inv = 1.0 / spread
    stat[0] = jnp.broadcast_to(centre, (own, 128))
    stat[1] = jnp.broadcast_to(inv, (own, 128))
    taps_per = 9 // PIECES
    for k in range(PIECES):
        for n in range(k * taps_per, (k + 1) * taps_per):
            w[rows_of(r), n * cin : (n + 1) * cin] = ((wraw[n].astype(F32) - centre) * inv).astype(BF)

        @pl.when(r < tall - 1)
        def _():
            w_copy(r, k, 0).start()

        @pl.when(r > 0)
        def _():
            w_copy(r, k, 1).start()

    for j in range(len(order)):
        img_copy(j, 0, p).start()

    def pass_on(s, k):
        up, dn = r - s, r + s

        @pl.when(inside & (up >= 0))
        def _():
            wait_in(w.at[rows_of(up), cols_of(k)], w_recv.at[up, k])
            w_copy(up, k, 0).start()

        @pl.when(inside & (dn <= tall - 1))
        def _():
            wait_in(w.at[rows_of(dn), cols_of(k)], w_recv.at[dn, k])
            w_copy(dn, k, 1).start()

    def w_wait_end(b):
        @pl.when(at_end)
        def _():
            for k in range(PIECES):
                wait_in(w.at[rows_of(b), cols_of(k)], w_recv.at[b, k])

    load_t.wait()
    want = goal_raw[...].reshape(px, goal_raw.shape[2])
    wide = goal_raw.shape[2]
    line = lax.broadcasted_iota(jnp.int32, (filters, wide), 0)
    chan = lax.broadcasted_iota(jnp.int32, (filters, wide), 1)
    first = (line // own) * (own * WIDE) + line % own
    for t in range(WIDE):
        pick = jnp.where(chan == first + t * own, 1.0, 0.0).astype(BF)
        goal[t] = dot(pick, want, NT).astype(BF)

    def half_rows(h):
        return pl.ds(pl.multiple_of(h * hf, hf), hf)

    def tgt_copy(h, k, to_f, to):
        return rc(
            goal.at[to_f, half_rows(h)], tg.at[f, half_rows(h)],
            t_send.at[k, h], t_recv.at[f, h], to,
        )

    near_half, far_half = flip, 1 - flip
    crossing = (u + 1) // mid
    soon = flip + crossing * (1 - 2 * flip)
    later = 1 - soon
    tgt_copy(soon, 0, fp, p).start()
    tgt_copy(later, 0, fp, p).start()
    tg[f] = goal[f]

    ii = lax.broadcasted_iota(jnp.int32, (2 * half, 2 * half), 0)
    jj = lax.broadcasted_iota(jnp.int32, (2 * half, 2 * half), 1)
    spread_out = jnp.where(jj == 2 * (ii % half) + ii // half, 1.0, 0.0).astype(BF)
    gather_in = jnp.where(ii == 2 * (jj % half) + jj // half, 1.0, 0.0).astype(BF)

    def split_one(index, at, block_img):
        v = dot(spread_out, block_img, NN).astype(BF)
        x[index, at : at + half, :one] = v[:half]
        x[index, at : at + half, one:] = v[half:]

    def split_pair(index, i0, a, b):
        split_one(index, i0 * half, a)
        split_one(index, (i0 + 1) * half, b)
        va = dot(a, gather_in, TN).astype(BF)
        vb = dot(b, gather_in, TN).astype(BF)
        lanes = slice(i0 * half, (i0 + 2) * half)
        xt[index, :one, lanes] = jnp.concatenate([va[:, :half], vb[:, :half]], axis=1)
        xt[index, one:, lanes] = jnp.concatenate([va[:, half:], vb[:, half:]], axis=1)

    def split_row(t, row):
        for i0 in range(0, imgs, 2):
            split_pair(1 + 2 * t + row, i0, raw[t, i0, row], raw[t, i0 + 1, row])

    def img_step(j):
        img_wait(fq, j)
        fwd_copy(j).start()

    def rim_step():
        @pl.when(r > 0)
        def _():
            wait_in(share, r_recv.at[0])
            rim_to_p.start()
            wait_in(other, r_recv.at[1])

    pass_on(1, 0)
    load_x.wait()
    for row in range(2):
        split_row(f, row)
    img_step(0)
    for j in range(len(order)):
        img_wait(fp, j)
    for row in range(2):
        split_row(fp, row)
    img_step(1)
    img_wait(fd, 0)
    img_wait(fd, 1)

    @pl.when((f < WIDE - 1) & (r < tall - 1))
    def _():
        rim_via.start()

    pass_on(1, 1)
    pass_on(1, 2)
    split_row(fq, 1)
    split_row(fd, 1)
    for h in range(2):
        wait_in(tg.at[fp, half_rows(h)], t_recv.at[fp, h])

    place = lax.broadcasted_iota(jnp.int32, (own, px), 1) % half

    def forward(b, tiles):
        rows = rows_of(b)
        for t in tiles:
            even = jnp.zeros((own, px), F32)
            odd = jnp.zeros((2 * own, px), F32)
            for kh in range(3):
                c = kh * three
                even += dot(w[rows, c + one : c + two], xt[2 * t + kh, :one], NN)
                both = jnp.concatenate([w[rows, c + two : c + three], w[rows, c : c + one]], axis=0)
                odd += dot(both, xt[2 * t + kh, one:], NN)
            left = jnp.where(place == 0, 0.0, pltpu.roll(odd[own:], 1, 1))
            out = even + odd[:own] + left
            grad = ((out - tg[t, rows].astype(F32)) * GRAD_SCALE).astype(BF)
            nxt = jnp.where(place == half - 1, 0.0, pltpu.roll(grad.astype(F32), px - 1, 1))
            gt[t, rows] = grad
            gts[t, rows] = nxt.astype(BF)

    def filter_terms(b):
        rows = rows_of(b)
        lhs = [gt[t, rows] for t in range(WIDE)]
        both = [jnp.concatenate([gts[t, rows], lhs[t]], axis=0) for t in range(WIDE)]
        sums = jnp.zeros((own, one), F32)
        for kh in range(3):
            c = kh * three
            even = dot(lhs[0], x[kh, :, :one], NN)
            odd = dot(both[0], x[kh, :, one:], NN)
            for t in range(1, WIDE):
                even += dot(lhs[t], x[2 * t + kh, :, :one], NN)
                odd += dot(both[t], x[2 * t + kh, :, one:], NN)
            g[rows, c : c + one] = odd[:own]
            g[rows, c + one : c + two] = even
            g[rows, c + two : c + three] = odd[own:]
            sums += even + odd[:own] + odd[own:]
        mean = jnp.sum(sums, axis=1, keepdims=True) * (1.0 / fan)
        for n in range(9):
            lanes = slice(n * one, (n + 1) * one)
            g[rows, lanes] = g[rows, lanes] - mean

    def g_copy(way, b, k, to):
        at = (way, rows_of(b), strip_of(k))
        return rc(part_out.at[at], part_in.at[at], g_send.at[way, b, k], g_recv.at[way, b, k], to)

    def g_wait(way, b, k):
        wait_in(part_in.at[way, rows_of(b), strip_of(k)], g_recv.at[way, b, k])

    def g_first(b, k):
        rows, cols = rows_of(b), strip_of(k)
        part_out[flip, rows, cols] = g[rows, cols].astype(BF)
        g_copy(flip, b, k, ahead_dev).start()

    def g_relay(way, b, k, to):
        rows, cols = rows_of(b), strip_of(k)
        g_wait(way, b, k)
        part_out[way, rows, cols] = (g[rows, cols] + part_in[way, rows, cols].astype(F32)).astype(BF)
        g_copy(way, b, k, to).start()

    def relay_lead(n, k):
        @pl.when(inside & (n > u))
        def _():
            g_relay(flip, block(n), k, ahead_dev)

    def relay_trail(n, k):
        @pl.when(inside & (n < u))
        def _():
            g_relay(1 - flip, block(n), k, behind_dev)

    img_step(2)
    for k, (to_f, to) in ((1, (fq, q)), (2, (fd, d))):
        tgt_copy(soon, k, to_f, to).start()
    pass_on(2, 0)
    rim_step()

    @pl.when(r > 0)
    def _():
        for i0 in range(0, imgs, 2):
            split_pair(0, i0, rim_raw[i0], rim_raw[i0 + 1])

    @pl.when(r == 0)
    def _():
        x[0] = jnp.zeros((px, two), BF)
        xt[0] = jnp.zeros((two, px), BF)

    first_b = block(u + 1)
    w_wait_end(first_b)
    img_step(3)
    for k, (to_f, to) in ((1, (fq, q)), (2, (fd, d))):
        tgt_copy(later, k, to_f, to).start()
    pass_on(2, 1)
    forward(first_b, (f, fp))
    split_row(fq, 0)
    img_wait(fd, 2)
    img_wait(fd, 3)
    split_row(fd, 0)
    pass_on(2, 2)
    for s in range(3, tall - 1):
        for k in range(PIECES):
            pass_on(s, k)
    for t in (fq, fd):
        wait_in(tg.at[t, half_rows(soon)], t_recv.at[t, soon])

    def turn(it, carry):
        i = jnp.where(it < 2, it + 1, jnp.where(it == 2, 0, it))
        n = nth(i)
        b = block(n)

        @pl.when((it == 1) | (it > 2))
        def _():
            w_wait_end(b)

        @pl.when(it == 1)
        def _():
            for t in (fq, fd):
                wait_in(tg.at[t, half_rows(later)], t_recv.at[t, later])

        @pl.when(it > 0)
        def _():
            forward(b, (f, fp))

        forward(b, (fq, fd))
        filter_terms(b)

        @pl.when(at_end & (n == 1))
        def _():
            for k in range(START):
                g_first(b, k)

        @pl.when(at_end & (n > 1))
        def _():
            for k in range(STRIPS):
                g_first(b, k)

        return carry

    lax.fori_loop(0, tall - 1, turn, 0)

    def turned(h):
        lanes = half_rows(h)
        for t in range(WIDE):
            gy[t, :, lanes] = gt[t, lanes].astype(F32).T.astype(BF)
            gys[t, :, lanes] = gts[t, lanes].astype(F32).T.astype(BF)

    gy[WIDE] = jnp.zeros((px, filters), BF)
    gys[WIDE] = jnp.zeros((px, filters), BF)
    turned(near_half)
    relay_lead(2, 0)
    relay_lead(2, 1)
    last_n = tall - 1
    last_b = block(last_n)
    w_wait_end(last_b)
    forward(last_b, (f, fp))
    forward(last_b, (fq, fd))
    turned(far_half)
    relay_lead(2, 2)
    relay_lead(2, 3)

    def taps(t, kh):
        c = kh * three
        even = dot(gy[t], w[:, c + one : c + two], NN)
        odd = dot(gy[t], w[:, c + two : c + three], NN)
        odd += dot(gys[t], w[:, c : c + one], NN)
        return even, odd

    def tile_row(t, row):
        if row == 0:
            return taps(t, 1)
        even, odd = taps(t, 2)
        more_even, more_odd = taps(t + 1, 0)
        return even + more_even, odd + more_odd

    halves = (slice(0, one), slice(one, two))
    half_px = px // 2
    keep = pl.ds(pl.multiple_of(c * half_px, half_px), half_px)
    give = pl.ds(pl.multiple_of((1 - c) * half_px, half_px), half_px)
    rim_pc = rc(rim_x.at[give], rim_p, e_send.at[0], e_recv.at[0], p)
    rim_zc = rc(rim_s, rim_z.at[keep], e_send.at[1], e_recv.at[1 + c], above + 1 - c)

    def rim_zwait():
        for n in range(2):
            part = slice(n * half_px, (n + 1) * half_px)
            wait_in(rim_z.at[part], e_recv.at[1 + n])

    def p_copy(k, row):
        at = (k, row)
        return rc(to_p.at[at], from_p.at[at], d_send.at[at], d_recv.at[at], p)

    def q_copy(row):
        return rc(to_q.at[row], from_q.at[row], d_send.at[2, row], d_recv.at[2, row], q)

    def for_p(k, t):
        for row in range(2):
            for part, lanes in zip(tile_row(t, row), halves):
                to_p[k, row, :, lanes] = part.astype(BF)
            p_copy(k, row).start()

    def for_q(row):
        sums = tile_row(fq, row)
        wait_in(from_p.at[1, row], d_recv.at[1, row])
        for part, lanes in zip(sums, halves):
            acc[row, :, lanes] = part + from_p[1, row, :, lanes].astype(F32)

    @pl.when(r > 0)
    def _():
        edge = taps(0, 0)
        for part, lanes in zip(edge, halves):
            rim_x[:, lanes] = part.astype(BF)
        rim_pc.start()

    for_p(1, fd)
    relay_lead(2, 4)
    relay_lead(2, 5)

    @pl.when(r > 0)
    def _():
        wait_in(rim_p, e_recv.at[0])
        rim_s[...] = (rim_x[keep].astype(F32) + rim_p[...].astype(F32)).astype(BF)
        rim_zc.start()

    for_q(0)
    to_q[0] = acc[0].astype(BF)
    q_copy(0).start()
    filter_terms(last_b)

    @pl.when(at_end)
    def _():
        for k in range(STRIPS):
            g_first(last_b, k)
        for k in range(START, STRIPS):
            g_first(first_b, k)

    for_q(1)
    for_p(0, fp)
    relay_lead(3, 0)
    relay_lead(3, 1)

    @pl.when((f == 1) & (r < tall - 1))
    def _():
        rim_zwait()
        acc[1] += rim_z[...].astype(F32)

    to_q[1] = acc[1].astype(BF)
    q_copy(1).start()
    relay_lead(3, 2)
    relay_trail(tall - 4, 0)
    for k in range(3, STRIPS):
        relay_lead(3, k)
        relay_trail(tall - 4, k - 2)
    relay_trail(tall - 4, STRIPS - 2)
    relay_trail(tall - 4, STRIPS - 1)

    def relays(t, carry):
        for k in range(STRIPS):
            relay_lead(t, k)
            relay_trail(tall - 1 - t, k)
        return carry

    if tall > 4:
        lax.fori_loop(4, tall, relays, 0)

    def out_row(row):
        return pltpu.make_async_copy(dout.at[:, row], dout_hbm.at[:, row], o_sem.at[row])

    for row in range(2):
        for part, lanes in zip(tile_row(f, row), halves):
            acc[row, :, lanes] = part
        wait_in(from_p.at[0, row], d_recv.at[0, row])
        acc[row] += from_p[0, row].astype(F32)

    @pl.when((r < tall - 1) & (f == 3))
    def _():
        rim_zwait()
        acc[1] += rim_z[...].astype(F32)

    def finish_row(row):
        wait_in(from_q.at[row], d_recv.at[2, row])
        total = (acc[row] + from_q[row].astype(F32)).astype(BF)
        for i in range(imgs):
            mine = total[i * half : (i + 1) * half]
            stacked = jnp.concatenate([mine[:, :one], mine[:, one:]], axis=0)
            dout[i, row] = dot(gather_in, stacked, NN).astype(BF)
        out_row(row).start()

    finish_row(0)

    mine = rows_of(r)

    @pl.when(r > 0)
    def _():
        for k in range(STRIPS):
            g_wait(0, r, k)
        g[mine] += part_in[0, mine].astype(F32)

    @pl.when(r < tall - 1)
    def _():
        for k in range(STRIPS):
            g_wait(1, r, k)
        g[mine] += part_in[1, mine].astype(F32)

    centre = stat[0][:, :1]
    inv = stat[1][:, :1]
    s1 = jnp.zeros((own, cin), F32)
    s2 = jnp.zeros((own, cin), F32)
    for n in range(9):
        hat = (wraw[n].astype(F32) - centre) * inv
        piece = g[mine, n * cin : (n + 1) * cin]
        s1 += piece
        s2 += piece * hat
    m1 = jnp.sum(s1, axis=1, keepdims=True) * (1.0 / fan)
    m2 = jnp.sum(s2, axis=1, keepdims=True) * (1.0 / fan)
    for n in range(9):
        hat = (wraw[n].astype(F32) - centre) * inv
        piece = g[mine, n * cin : (n + 1) * cin]
        gout[n] = (piece - m1 - hat * m2) * inv
    out_g = pltpu.make_async_copy(gout, gout_hbm, o_sem.at[2])
    out_g.start()
    finish_row(1)

    for j in range(len(order)):
        img_copy(j, 0, p).wait_send()
        img_copy(j, 1, q).wait_send()
        fwd_copy(j).wait_send()
    for h in range(2):
        tgt_copy(h, 0, fp, p).wait_send()
        tgt_copy(h, 1, fq, q).wait_send()
        tgt_copy(h, 2, fd, d).wait_send()
    for row in range(2):
        p_copy(0, row).wait_send()
        p_copy(1, row).wait_send()
        q_copy(row).wait_send()

    @pl.when(r < tall - 1)
    def _():
        rim_in.wait_send()

    @pl.when(r > 0)
    def _():
        rim_to_p.wait_send()

    @pl.when(r > 0)
    def _():
        rim_pc.wait_send()
        rim_zc.wait_send()

    def drain(b, carry):
        for k in range(PIECES):
            @pl.when((r < tall - 1) & (b <= r))
            def _():
                w_copy(b, k, 0).wait_send()

            @pl.when((r > 0) & (b >= r))
            def _():
                w_copy(b, k, 1).wait_send()

        for k in range(STRIPS):
            @pl.when(b > r)
            def _():
                g_copy(0, b, k, p).wait_send()

            @pl.when(b < r)
            def _():
                g_copy(1, b, k, p).wait_send()

        return carry

    lax.fori_loop(0, tall, drain, 0)
    out_g.wait()
    for row in range(2):
        out_row(row).wait()


def shards(images, target, raw_filters):
    imgs, two_rows, in_cols, cin = images.shape
    half = in_cols // 2
    own = raw_filters.shape[0]
    tall = lax.axis_size("space") // WIDE
    fan = 9 * cin
    px = imgs * half
    filters = tall * own
    wide = target.shape[3]
    vm = pltpu.VMEM
    dma = pltpu.SemaphoreType.DMA
    row = (px, 2 * cin)
    scratch = [
        vm(images.shape, BF), vm((9, own, cin), F32),
        vm((WIDE,) + images.shape, BF), vm((imgs, in_cols, cin), BF), vm((imgs, half, wide), BF),
        vm((9, own, cin), BF), vm((2, own, 128), F32),
        vm((2 * WIDE + 1,) + row, BF), vm((2 * WIDE + 1, 2 * cin, px), BF), vm((filters, fan), BF),
        vm((WIDE, filters, px), BF), vm((WIDE, filters, px), BF),
        vm((WIDE + 1, px, filters), BF), vm((WIDE + 1, px, filters), BF),
        vm((WIDE, filters, px), BF), vm((WIDE, filters, px), BF), vm((filters, fan), F32),
        vm((2, filters, fan), BF), vm((2, filters, fan), BF),
        vm((2, 2) + row, BF), vm((2, 2) + row, BF), vm((2,) + row, BF), vm((2,) + row, BF),
        vm((2,) + row, F32),
        vm(row, BF), vm((px // 2, 2 * cin), BF), vm((px // 2, 2 * cin), BF), vm(row, BF),
        dma((3,)), dma((3,)), dma((WIDE, 4)), dma((3, 4)), dma((tall, PIECES)), dma((2, tall, PIECES)),
        dma((WIDE, 2)), dma((3, 2)), dma((2,)), dma((2,)),
        dma((2, tall, STRIPS)), dma((2, tall, STRIPS)), dma((3, 2)), dma((3, 2)), dma((3,)), dma((2,)),
    ]
    input_grads, by_tap = pl.pallas_call(
        functools.partial(kernel, tall, own, half, cin),
        out_shape=(
            jax.ShapeDtypeStruct(images.shape, BF),
            jax.ShapeDtypeStruct((9, own, cin), F32),
        ),
        in_specs=[pl.BlockSpec(memory_space=pl.ANY)] * 3,
        out_specs=[pl.BlockSpec(memory_space=pl.ANY)] * 2,
        scratch_shapes=scratch,
        compiler_params=pltpu.CompilerParams(
            collective_id=0, has_side_effects=True, vmem_limit_bytes=60 * 1024 * 1024
        ),
        name="tiles",
    )(
        images,
        target.reshape(imgs, half, wide),
        raw_filters.transpose(1, 2, 0, 3).reshape(9, own, cin),
    )
    filter_grads = by_tap.reshape(3, 3, own, cin).transpose(2, 0, 1, 3)
    return (input_grads, filter_grads)


def solution(mesh):
    return jax.shard_map(
        shards,
        mesh=mesh,
        in_specs=(
            P("parts", "space", None, None),
            P("parts", "space", None, None),
            P(("parts", "space"), None, None, None),
        ),
        out_specs=(P("parts", "space", None, None), P(("parts", "space"), None, None, None)),
        check_vma=False,
    )
```

```python
import functools

import jax
import jax.numpy as jnp
from jax import lax
from jax.experimental import pallas as pl
from jax.experimental.pallas import tpu as pltpu
from jax.sharding import PartitionSpec as P

EPS = 1e-05
GRAD_SCALE = 0.015625
WIDE = 4
PIECES = 3
STRIPS = 9
START = (3, 4)
F32 = jnp.float32
BF = jnp.bfloat16
NT = (((1,), (1,)), ((), ()))
NN = (((1,), (0,)), ((), ()))
TN = (((0,), (0,)), ((), ()))
MESH = pl.DeviceIdType.MESH


def dot(a, b, dims):
    return lax.dot_general(a, b, dims, preferred_element_type=F32)


def kernel(
    tall, own, half, cin,
    images, target, filters_in, dout, gout,
    raw, rim_raw, goal_raw, wraw, stat,
    x, xt, w, goal, tg, gy, gys, gt, gts, g, part_in, part_out,
    to_p, from_p, to_q, from_q, acc, rim_x, rim_p, rim_s, rim_z,
    l_sem, i_recv, i_send, w_recv, w_send, t_recv, t_send, r_recv, r_send,
    g_recv, g_send, d_recv, d_send, e_recv, e_send,
):
    me = lax.axis_index("space")
    r, f = me // WIDE, me % WIDE
    base = r * WIDE
    fp = f + 1 - 2 * (f % 2)
    fq = f + 2 - 4 * (f // 2)
    fd = fp + 2 - 4 * (fp // 2)
    p, q, d = base + fp, base + fq, base + fd
    above, below = me - WIDE, me + WIDE
    imgs = images.shape[0]
    px = imgs * half
    two, one = 2 * cin, cin
    three = 3 * cin
    filters = tall * own
    fan = 9 * cin
    mid = tall // 2
    hf = filters // 2
    flip = r // mid
    u = r + flip * (tall - 1 - 2 * r)
    ahead_dev = me + WIDE - 2 * WIDE * flip
    behind_dev = me - WIDE + 2 * WIDE * flip
    at_end = u == 0
    inside = u > 0

    def rc(src, dst, ssem, rsem, to):
        return pltpu.make_async_remote_copy(
            src_ref=src, dst_ref=dst, send_sem=ssem, recv_sem=rsem,
            device_id={"space": to}, device_id_type=MESH,
        )

    def wait_in(dst, rsem):
        rc(dst, dst, rsem, rsem, p).wait_recv()

    def rows_of(b):
        return pl.ds(pl.multiple_of(b * own, own), own)

    wide_cols = fan // PIECES

    def cols_of(k):
        return slice(k * wide_cols, (k + 1) * wide_cols)

    strip_cols = fan // STRIPS

    def strip_of(k):
        return slice(k * strip_cols, (k + 1) * strip_cols)

    def block(n):
        return n + flip * (tall - 1 - 2 * n)

    def nth(i):
        near = jnp.where(i % 2 == 1, u + (i + 1) // 2, u - i // 2)
        return jnp.where(i > 2 * u, i, near)

    bar = pltpu.get_barrier_semaphore()

    def greet(to):
        pl.semaphore_signal(bar, inc=1, device_id={"space": to}, device_id_type=MESH)

    for to in (p, q, d):
        greet(to)

    @pl.when(r > 0)
    def _():
        greet(above)

    @pl.when(r < tall - 1)
    def _():
        greet(below)

    load_w = pltpu.make_async_copy(filters_in, wraw, l_sem.at[0])
    load_x = pltpu.make_async_copy(images, raw.at[f], l_sem.at[1])
    load_t = pltpu.make_async_copy(target, goal_raw, l_sem.at[2])
    load_w.start()
    load_x.start()
    load_t.start()

    @pl.when((r < tall - 1) & (f % 2 == 1))
    def _():
        greet(below - 1)

    load_w.wait()
    centre = wraw[0].astype(F32)
    for k in range(1, 9):
        centre += wraw[k].astype(F32)
    centre = jnp.sum(centre, axis=1, keepdims=True) * (1.0 / fan)
    spread = jnp.zeros((own, cin), F32)
    for k in range(9):
        off = wraw[k].astype(F32) - centre
        spread += off * off
    spread = jnp.sqrt(jnp.sum(spread, axis=1, keepdims=True) * (1.0 / fan) + EPS)
    inv = 1.0 / spread
    stat[0] = jnp.broadcast_to(centre, (own, 128))
    stat[1] = jnp.broadcast_to(inv, (own, 128))
    for n in range(9):
        w[rows_of(r), n * cin : (n + 1) * cin] = ((wraw[n].astype(F32) - centre) * inv).astype(BF)

    more = (r > 0) & (f % 2 == 0)
    fewer = jnp.logical_not(more)

    @pl.when(inside & more)
    def _():
        pl.semaphore_wait(bar, 6)

    @pl.when((inside & fewer) | (at_end & more))
    def _():
        pl.semaphore_wait(bar, 5)

    @pl.when(at_end & fewer)
    def _():
        pl.semaphore_wait(bar, 4)

    pairs = 2
    per = imgs // pairs
    order = [(row, h) for row in (1, 0) for h in range(pairs)]

    def piece_of(ref, j):
        row, h = order[j]
        return ref.at[slice(h * per, (h + 1) * per), row]

    def img_copy(j, k, to):
        return rc(piece_of(images, j), piece_of(raw.at[f], j), i_send.at[k, j], i_recv.at[f, j], to)

    def fwd_copy(j):
        slot = piece_of(raw.at[fq], j)
        return rc(slot, slot, i_send.at[2, j], i_recv.at[fq, j], p)

    def img_wait(t, j):
        wait_in(piece_of(raw.at[t], j), i_recv.at[t, j])

    c = f % 2
    share = rim_raw.at[pl.ds(c * per, per)]
    other = rim_raw.at[pl.ds((1 - c) * per, per)]
    rim_in = rc(images.at[pl.ds(c * per, per), 1], share, r_send.at[0], r_recv.at[0], below)
    rim_via = rc(raw.at[WIDE - 1, pl.ds(c * per, per), 1], share, r_send.at[0], r_recv.at[0], below)
    rim_to_p = rc(share, share, r_send.at[1], r_recv.at[1], p)

    for j in range(len(order)):
        img_copy(j, 1, q).start()

    @pl.when((f == 3) & (r < tall - 1))
    def _():
        rim_in.start()

    def w_copy(b, k, way):
        slot = w.at[rows_of(b), cols_of(k)]
        to = below if way == 0 else above
        return rc(slot, slot, w_send.at[way, b, k], w_recv.at[b, k], to)

    for k in range(PIECES):
        @pl.when(r < tall - 1)
        def _():
            w_copy(r, k, 0).start()

        @pl.when(r > 0)
        def _():
            w_copy(r, k, 1).start()

    for j in range(len(order)):
        img_copy(j, 0, p).start()

    def pass_on(s, k):
        up, dn = r - s, r + s

        @pl.when(inside & (up >= 0))
        def _():
            wait_in(w.at[rows_of(up), cols_of(k)], w_recv.at[up, k])
            w_copy(up, k, 0).start()

        @pl.when(inside & (dn <= tall - 1))
        def _():
            wait_in(w.at[rows_of(dn), cols_of(k)], w_recv.at[dn, k])
            w_copy(dn, k, 1).start()

    def w_wait_end(b):
        @pl.when(at_end)
        def _():
            for k in range(PIECES):
                wait_in(w.at[rows_of(b), cols_of(k)], w_recv.at[b, k])

    load_t.wait()
    want = goal_raw[...].reshape(px, goal_raw.shape[2])
    wide = goal_raw.shape[2]
    line = lax.broadcasted_iota(jnp.int32, (filters, wide), 0)
    chan = lax.broadcasted_iota(jnp.int32, (filters, wide), 1)
    first = (line // own) * (own * WIDE) + line % own
    for t in range(WIDE):
        pick = jnp.where(chan == first + t * own, 1.0, 0.0).astype(BF)
        goal[t] = dot(pick, want, NT).astype(BF)

    def half_rows(h):
        return pl.ds(pl.multiple_of(h * hf, hf), hf)

    def tgt_copy(h, k, to_f, to):
        return rc(
            goal.at[to_f, half_rows(h)], tg.at[f, half_rows(h)],
            t_send.at[k, h], t_recv.at[f, h], to,
        )

    near_half, far_half = flip, 1 - flip
    crossing = (u + 1) // mid
    soon = flip + crossing * (1 - 2 * flip)
    later = 1 - soon
    tgt_copy(soon, 0, fp, p).start()
    tgt_copy(later, 0, fp, p).start()
    tg[f] = goal[f]

    ii = lax.broadcasted_iota(jnp.int32, (2 * half, 2 * half), 0)
    jj = lax.broadcasted_iota(jnp.int32, (2 * half, 2 * half), 1)
    spread_out = jnp.where(jj == 2 * (ii % half) + ii // half, 1.0, 0.0).astype(BF)
    gather_in = jnp.where(ii == 2 * (jj % half) + jj // half, 1.0, 0.0).astype(BF)

    def split_one(index, at, block_img):
        v = dot(spread_out, block_img, NN).astype(BF)
        x[index, at : at + half, :one] = v[:half]
        x[index, at : at + half, one:] = v[half:]

    def split_pair(index, i0, a, b):
        split_one(index, i0 * half, a)
        split_one(index, (i0 + 1) * half, b)
        va = dot(a, gather_in, TN).astype(BF)
        vb = dot(b, gather_in, TN).astype(BF)
        lanes = slice(i0 * half, (i0 + 2) * half)
        xt[index, :one, lanes] = jnp.concatenate([va[:, :half], vb[:, :half]], axis=1)
        xt[index, one:, lanes] = jnp.concatenate([va[:, half:], vb[:, half:]], axis=1)

    def split_row(t, row):
        for i0 in range(0, imgs, 2):
            split_pair(1 + 2 * t + row, i0, raw[t, i0, row], raw[t, i0 + 1, row])

    def img_step(j):
        img_wait(fq, j)
        fwd_copy(j).start()

    def rim_step():
        @pl.when(r > 0)
        def _():
            wait_in(share, r_recv.at[0])
            rim_to_p.start()
            wait_in(other, r_recv.at[1])

    pass_on(1, 0)
    load_x.wait()
    for row in range(2):
        split_row(f, row)
    img_step(0)
    for j in range(len(order)):
        img_wait(fp, j)
    for row in range(2):
        split_row(fp, row)
    img_step(1)
    img_wait(fd, 0)
    img_wait(fd, 1)

    @pl.when((f < WIDE - 1) & (r < tall - 1))
    def _():
        rim_via.start()

    pass_on(1, 1)
    pass_on(1, 2)
    split_row(fq, 1)
    split_row(fd, 1)
    for h in range(2):
        wait_in(tg.at[fp, half_rows(h)], t_recv.at[fp, h])

    place = lax.broadcasted_iota(jnp.int32, (own, px), 1) % half

    def forward(b, tiles):
        rows = rows_of(b)
        for t in tiles:
            even = jnp.zeros((own, px), F32)
            odd = jnp.zeros((2 * own, px), F32)
            for kh in range(3):
                c = kh * three
                even += dot(w[rows, c + one : c + two], xt[2 * t + kh, :one], NN)
                both = jnp.concatenate([w[rows, c + two : c + three], w[rows, c : c + one]], axis=0)
                odd += dot(both, xt[2 * t + kh, one:], NN)
            left = jnp.where(place == 0, 0.0, pltpu.roll(odd[own:], 1, 1))
            out = even + odd[:own] + left
            grad = ((out - tg[t, rows].astype(F32)) * GRAD_SCALE).astype(BF)
            nxt = jnp.where(place == half - 1, 0.0, pltpu.roll(grad.astype(F32), px - 1, 1))
            gt[t, rows] = grad
            gts[t, rows] = nxt.astype(BF)

    def filter_terms(b):
        rows = rows_of(b)
        lhs = [gt[t, rows] for t in range(WIDE)]
        both = [jnp.concatenate([gts[t, rows], lhs[t]], axis=0) for t in range(WIDE)]
        sums = jnp.zeros((own, one), F32)
        for kh in range(3):
            c = kh * three
            even = dot(lhs[0], x[kh, :, :one], NN)
            odd = dot(both[0], x[kh, :, one:], NN)
            for t in range(1, WIDE):
                even += dot(lhs[t], x[2 * t + kh, :, :one], NN)
                odd += dot(both[t], x[2 * t + kh, :, one:], NN)
            g[rows, c : c + one] = odd[:own]
            g[rows, c + one : c + two] = even
            g[rows, c + two : c + three] = odd[own:]
            sums += even + odd[:own] + odd[own:]
        mean = jnp.sum(sums, axis=1, keepdims=True) * (1.0 / fan)
        for n in range(9):
            lanes = slice(n * one, (n + 1) * one)
            g[rows, lanes] = g[rows, lanes] - mean

    def g_copy(way, b, k, to):
        at = (way, rows_of(b), strip_of(k))
        return rc(part_out.at[at], part_in.at[at], g_send.at[way, b, k], g_recv.at[way, b, k], to)

    def g_wait(way, b, k):
        wait_in(part_in.at[way, rows_of(b), strip_of(k)], g_recv.at[way, b, k])

    def g_first(b, k):
        rows, cols = rows_of(b), strip_of(k)
        part_out[flip, rows, cols] = g[rows, cols].astype(BF)
        g_copy(flip, b, k, ahead_dev).start()

    def g_relay(way, b, k, to):
        rows, cols = rows_of(b), strip_of(k)
        g_wait(way, b, k)
        part_out[way, rows, cols] = (g[rows, cols] + part_in[way, rows, cols].astype(F32)).astype(BF)
        g_copy(way, b, k, to).start()

    def relay_lead(n, k):
        @pl.when(inside & (n > u))
        def _():
            g_relay(flip, block(n), k, ahead_dev)

    def relay_trail(n, k):
        @pl.when(inside & (n < u))
        def _():
            g_relay(1 - flip, block(n), k, behind_dev)

    img_step(2)
    for k, (to_f, to) in ((1, (fq, q)), (2, (fd, d))):
        tgt_copy(soon, k, to_f, to).start()
    pass_on(2, 0)
    rim_step()

    @pl.when(r > 0)
    def _():
        for i0 in range(0, imgs, 2):
            split_pair(0, i0, rim_raw[i0], rim_raw[i0 + 1])

    @pl.when(r == 0)
    def _():
        x[0] = jnp.zeros((px, two), BF)
        xt[0] = jnp.zeros((two, px), BF)

    first_b = block(u + 1)
    w_wait_end(first_b)
    img_step(3)
    for k, (to_f, to) in ((1, (fq, q)), (2, (fd, d))):
        tgt_copy(later, k, to_f, to).start()
    pass_on(2, 1)
    forward(first_b, (f, fp))
    split_row(fq, 0)
    img_wait(fd, 2)
    img_wait(fd, 3)
    split_row(fd, 0)
    pass_on(2, 2)
    for s in range(3, tall - 1):
        for k in range(PIECES):
            pass_on(s, k)
    for t in (fq, fd):
        wait_in(tg.at[t, half_rows(soon)], t_recv.at[t, soon])

    def turn(it, carry):
        i = jnp.where(it < 2, it + 1, jnp.where(it == 2, 0, it))
        n = nth(i)
        b = block(n)

        @pl.when((it == 1) | (it > 2))
        def _():
            w_wait_end(b)

        @pl.when(it == 1)
        def _():
            for t in (fq, fd):
                wait_in(tg.at[t, half_rows(later)], t_recv.at[t, later])

        @pl.when(it > 0)
        def _():
            forward(b, (f, fp))

        forward(b, (fq, fd))
        filter_terms(b)

        @pl.when(at_end & (n == 1))
        def _():
            for k in range(START[0]):
                g_first(b, k)

            @pl.when(flip == 1)
            def _():
                for k in range(START[0], START[1]):
                    g_first(b, k)

        @pl.when(at_end & (n > 1))
        def _():
            for k in range(STRIPS):
                g_first(b, k)

        return carry

    lax.fori_loop(0, tall - 1, turn, 0)

    def turned(h):
        lanes = half_rows(h)
        for t in range(WIDE):
            gy[t, :, lanes] = gt[t, lanes].astype(F32).T.astype(BF)
            gys[t, :, lanes] = gts[t, lanes].astype(F32).T.astype(BF)

    gy[WIDE] = jnp.zeros((px, filters), BF)
    gys[WIDE] = jnp.zeros((px, filters), BF)
    turned(near_half)
    for k in range(3):
        relay_lead(2, k)
    last_n = tall - 1
    last_b = block(last_n)
    w_wait_end(last_b)
    forward(last_b, (f, fp))
    forward(last_b, (fq, fd))
    turned(far_half)
    for k in range(3, 6):
        relay_lead(2, k)

    def taps(t, kh):
        c = kh * three
        even = dot(gy[t], w[:, c + one : c + two], NN)
        odd = dot(gy[t], w[:, c + two : c + three], NN)
        odd += dot(gys[t], w[:, c : c + one], NN)
        return even, odd

    def tile_row(t, row):
        if row == 0:
            return taps(t, 1)
        even, odd = taps(t, 2)
        more_even, more_odd = taps(t + 1, 0)
        return even + more_even, odd + more_odd

    halves = (slice(0, one), slice(one, two))
    half_px = px // 2
    keep = pl.ds(pl.multiple_of(c * half_px, half_px), half_px)
    give = pl.ds(pl.multiple_of((1 - c) * half_px, half_px), half_px)
    rim_pc = rc(rim_x.at[give], rim_p, e_send.at[0], e_recv.at[0], p)
    rim_zc = rc(rim_s, rim_z.at[keep], e_send.at[1], e_recv.at[1 + c], above + 1 - c)

    def rim_zwait():
        for n in range(2):
            part = slice(n * half_px, (n + 1) * half_px)
            wait_in(rim_z.at[part], e_recv.at[1 + n])

    def p_copy(k, row):
        at = (k, row)
        return rc(to_p.at[at], from_p.at[at], d_send.at[at], d_recv.at[at], p)

    def q_copy(row):
        return rc(to_q.at[row], from_q.at[row], d_send.at[2, row], d_recv.at[2, row], q)

    def for_p(k, t):
        for row in range(2):
            for part, lanes in zip(tile_row(t, row), halves):
                to_p[k, row, :, lanes] = part.astype(BF)
            p_copy(k, row).start()

    def for_q(row):
        sums = tile_row(fq, row)
        wait_in(from_p.at[1, row], d_recv.at[1, row])
        for part, lanes in zip(sums, halves):
            acc[row, :, lanes] = part + from_p[1, row, :, lanes].astype(F32)

    @pl.when(r > 0)
    def _():
        edge = taps(0, 0)
        for part, lanes in zip(edge, halves):
            rim_x[:, lanes] = part.astype(BF)
        rim_pc.start()

    for_p(1, fd)
    for k in range(6, STRIPS):
        relay_lead(2, k)

    @pl.when(r > 0)
    def _():
        wait_in(rim_p, e_recv.at[0])
        rim_s[...] = (rim_x[keep].astype(F32) + rim_p[...].astype(F32)).astype(BF)
        rim_zc.start()

    filter_terms(last_b)

    @pl.when(at_end)
    def _():
        for k in range(STRIPS):
            g_first(last_b, k)

        @pl.when(flip == 0)
        def _():
            for k in range(START[0], START[1]):
                g_first(first_b, k)

        for k in range(START[1], STRIPS):
            g_first(first_b, k)

    for_q(0)
    to_q[0] = acc[0].astype(BF)
    q_copy(0).start()
    for_q(1)
    for_p(0, fp)
    relay_lead(3, 0)
    relay_lead(3, 1)

    @pl.when((f == 1) & (r < tall - 1))
    def _():
        rim_zwait()
        acc[1] += rim_z[...].astype(F32)

    to_q[1] = acc[1].astype(BF)
    q_copy(1).start()

    def both_ways(lag):
        for k in range(2, STRIPS + lag):
            if k < STRIPS:
                relay_lead(3, k)
            if k >= lag:
                relay_trail(tall - 4, k - lag)

    @pl.when(flip == 0)
    def _():
        both_ways(6)

    @pl.when(flip == 1)
    def _():
        both_ways(2)

    def relays(t, carry):
        for k in range(STRIPS):
            relay_lead(t, k)
            relay_trail(tall - 1 - t, k)
        return carry

    if tall > 4:
        lax.fori_loop(4, tall, relays, 0)

    for row in range(2):
        for part, lanes in zip(tile_row(f, row), halves):
            acc[row, :, lanes] = part
        wait_in(from_p.at[0, row], d_recv.at[0, row])
        acc[row] += from_p[0, row].astype(F32)

    @pl.when((r < tall - 1) & (f == 3))
    def _():
        rim_zwait()
        acc[1] += rim_z[...].astype(F32)

    def finish_row(row):
        wait_in(from_q.at[row], d_recv.at[2, row])
        total = (acc[row] + from_q[row].astype(F32)).astype(BF)
        for i in range(imgs):
            mine = total[i * half : (i + 1) * half]
            stacked = jnp.concatenate([mine[:, :one], mine[:, one:]], axis=0)
            dout[i, row] = dot(gather_in, stacked, NN).astype(BF)

    finish_row(0)
    finish_row(1)

    mine = rows_of(r)
    centre = stat[0][:, :1]
    inv = stat[1][:, :1]
    s1 = jnp.zeros((own, cin), F32)
    s2 = jnp.zeros((own, cin), F32)
    for k in range(STRIPS):
        cols = strip_of(k)

        @pl.when(r > 0)
        def _():
            g_wait(0, r, k)
            g[mine, cols] += part_in[0, mine, cols].astype(F32)

        @pl.when(r < tall - 1)
        def _():
            g_wait(1, r, k)
            g[mine, cols] += part_in[1, mine, cols].astype(F32)

        piece = g[mine, cols]
        s1 += piece
        s2 += piece * ((wraw[k].astype(F32) - centre) * inv)
    m1 = jnp.sum(s1, axis=1, keepdims=True) * (1.0 / fan)
    m2 = jnp.sum(s2, axis=1, keepdims=True) * (1.0 / fan)
    for n in range(9):
        hat = (wraw[n].astype(F32) - centre) * inv
        gout[n] = (g[mine, strip_of(n)] - m1 - hat * m2) * inv

    for j in range(len(order)):
        img_copy(j, 0, p).wait_send()
        img_copy(j, 1, q).wait_send()
        fwd_copy(j).wait_send()
    for h in range(2):
        tgt_copy(h, 0, fp, p).wait_send()
        tgt_copy(h, 1, fq, q).wait_send()
        tgt_copy(h, 2, fd, d).wait_send()
    for row in range(2):
        p_copy(0, row).wait_send()
        p_copy(1, row).wait_send()
        q_copy(row).wait_send()

    @pl.when(r < tall - 1)
    def _():
        rim_in.wait_send()

    @pl.when(r > 0)
    def _():
        rim_to_p.wait_send()

    @pl.when(r > 0)
    def _():
        rim_pc.wait_send()
        rim_zc.wait_send()

    def drain(b, carry):
        for k in range(PIECES):
            @pl.when((r < tall - 1) & (b <= r))
            def _():
                w_copy(b, k, 0).wait_send()

            @pl.when((r > 0) & (b >= r))
            def _():
                w_copy(b, k, 1).wait_send()

        for k in range(STRIPS):
            @pl.when(b > r)
            def _():
                g_copy(0, b, k, p).wait_send()

            @pl.when(b < r)
            def _():
                g_copy(1, b, k, p).wait_send()

        return carry

    lax.fori_loop(0, tall, drain, 0)


def shards(images, target, raw_filters):
    imgs, two_rows, in_cols, cin = images.shape
    half = in_cols // 2
    own = raw_filters.shape[0]
    tall = lax.axis_size("space") // WIDE
    fan = 9 * cin
    px = imgs * half
    filters = tall * own
    wide = target.shape[3]
    vm = pltpu.VMEM
    dma = pltpu.SemaphoreType.DMA
    row = (px, 2 * cin)
    scratch = [
        vm((WIDE,) + images.shape, BF), vm((imgs, in_cols, cin), BF), vm((imgs, half, wide), BF),
        vm((9, own, cin), BF), vm((2, own, 128), F32),
        vm((2 * WIDE + 1,) + row, BF), vm((2 * WIDE + 1, 2 * cin, px), BF), vm((filters, fan), BF),
        vm((WIDE, filters, px), BF), vm((WIDE, filters, px), BF),
        vm((WIDE + 1, px, filters), BF), vm((WIDE + 1, px, filters), BF),
        vm((WIDE, filters, px), BF), vm((WIDE, filters, px), BF), vm((filters, fan), F32),
        vm((2, filters, fan), BF), vm((2, filters, fan), BF),
        vm((2, 2) + row, BF), vm((2, 2) + row, BF), vm((2,) + row, BF), vm((2,) + row, BF),
        vm((2,) + row, F32),
        vm(row, BF), vm((px // 2, 2 * cin), BF), vm((px // 2, 2 * cin), BF), vm(row, BF),
        dma((3,)), dma((WIDE, 4)), dma((3, 4)), dma((tall, PIECES)), dma((2, tall, PIECES)),
        dma((WIDE, 2)), dma((3, 2)), dma((2,)), dma((2,)),
        dma((2, tall, STRIPS)), dma((2, tall, STRIPS)), dma((3, 2)), dma((3, 2)), dma((3,)), dma((2,)),
    ]
    input_grads, by_tap = pl.pallas_call(
        functools.partial(kernel, tall, own, half, cin),
        out_shape=(
            pltpu.VMEM(images.shape, BF),
            pltpu.VMEM((9, own, cin), F32),
        ),
        in_specs=[pl.BlockSpec(memory_space=pl.ANY)] * 3,
        out_specs=[pl.BlockSpec(memory_space=pltpu.VMEM)] * 2,
        scratch_shapes=scratch,
        compiler_params=pltpu.CompilerParams(
            collective_id=0, has_side_effects=True, vmem_limit_bytes=56 * 1024 * 1024
        ),
        name="tiles",
    )(
        images,
        target.reshape(imgs, half, wide),
        raw_filters.transpose(1, 2, 0, 3).reshape(9, own, cin),
    )
    filter_grads = by_tap.reshape(3, 3, own, cin).transpose(2, 0, 1, 3)
    return (input_grads, filter_grads)


def solution(mesh):
    return jax.shard_map(
        shards,
        mesh=mesh,
        in_specs=(
            P("parts", "space", None, None),
            P("parts", "space", None, None),
            P(("parts", "space"), None, None, None),
        ),
        out_specs=(P("parts", "space", None, None), P(("parts", "space"), None, None, None)),
        check_vma=False,
    )
```

```python
import functools

import jax
import jax.numpy as jnp
from jax import lax
from jax.experimental import pallas as pl
from jax.experimental.pallas import tpu as pltpu
from jax.sharding import PartitionSpec as P

EPS = 1e-05
GRAD_SCALE = 0.015625
WIDE = 4
PIECES = 3
STRIPS = 9
START = (2, 3)
F32 = jnp.float32
BF = jnp.bfloat16
NT = (((1,), (1,)), ((), ()))
NN = (((1,), (0,)), ((), ()))
TN = (((0,), (0,)), ((), ()))
MESH = pl.DeviceIdType.MESH


def dot(a, b, dims):
    return lax.dot_general(a, b, dims, preferred_element_type=F32)


def kernel(
    tall, own, half, cin,
    images, target, filters_in, dout, gout,
    raw, rim_raw, goal_raw, wraw, stat,
    x, xt, w, goal, tg, gy, gys, gt, gts, g, part_in, part_out,
    to_p, from_p, to_q, from_q, acc, rim_x, rim_p, rim_s, rim_z,
    l_sem, i_recv, i_send, w_recv, w_send, t_recv, t_send, r_recv, r_send,
    g_recv, g_send, d_recv, d_send, e_recv, e_send,
):
    me = lax.axis_index("space")
    r, f = me // WIDE, me % WIDE
    base = r * WIDE
    fp = f + 1 - 2 * (f % 2)
    fq = f + 2 - 4 * (f // 2)
    fd = fp + 2 - 4 * (fp // 2)
    p, q, d = base + fp, base + fq, base + fd
    above, below = me - WIDE, me + WIDE
    imgs = images.shape[0]
    px = imgs * half
    two, one = 2 * cin, cin
    three = 3 * cin
    filters = tall * own
    fan = 9 * cin
    mid = tall // 2
    hf = filters // 2
    flip = r // mid
    u = r + flip * (tall - 1 - 2 * r)
    ahead_dev = me + WIDE - 2 * WIDE * flip
    behind_dev = me - WIDE + 2 * WIDE * flip
    at_end = u == 0
    inside = u > 0

    def rc(src, dst, ssem, rsem, to):
        return pltpu.make_async_remote_copy(
            src_ref=src, dst_ref=dst, send_sem=ssem, recv_sem=rsem,
            device_id={"space": to}, device_id_type=MESH,
        )

    def wait_in(dst, rsem):
        rc(dst, dst, rsem, rsem, p).wait_recv()

    def rows_of(b):
        return pl.ds(pl.multiple_of(b * own, own), own)

    wide_cols = fan // PIECES

    def cols_of(k):
        return slice(k * wide_cols, (k + 1) * wide_cols)

    strip_cols = fan // STRIPS

    def strip_of(k):
        return slice(k * strip_cols, (k + 1) * strip_cols)

    def block(n):
        return n + flip * (tall - 1 - 2 * n)

    def nth(i):
        near = jnp.where(i % 2 == 1, u + (i + 1) // 2, u - i // 2)
        return jnp.where(i > 2 * u, i, near)

    bar = pltpu.get_barrier_semaphore()

    def greet(to):
        pl.semaphore_signal(bar, inc=1, device_id={"space": to}, device_id_type=MESH)

    for to in (p, q, d):
        greet(to)

    @pl.when(r > 0)
    def _():
        greet(above)

    @pl.when(r < tall - 1)
    def _():
        greet(below)

    load_w = pltpu.make_async_copy(filters_in, wraw, l_sem.at[0])
    load_x = pltpu.make_async_copy(images, raw.at[f], l_sem.at[1])
    load_t = pltpu.make_async_copy(target, goal_raw, l_sem.at[2])
    load_w.start()
    load_x.start()
    load_t.start()

    @pl.when((r < tall - 1) & (f % 2 == 1))
    def _():
        greet(below - 1)

    load_w.wait()
    centre = wraw[0].astype(F32)
    for k in range(1, 9):
        centre += wraw[k].astype(F32)
    centre = jnp.sum(centre, axis=1, keepdims=True) * (1.0 / fan)
    spread = jnp.zeros((own, cin), F32)
    for k in range(9):
        off = wraw[k].astype(F32) - centre
        spread += off * off
    spread = jnp.sqrt(jnp.sum(spread, axis=1, keepdims=True) * (1.0 / fan) + EPS)
    inv = 1.0 / spread
    stat[0] = jnp.broadcast_to(centre, (own, 128))
    stat[1] = jnp.broadcast_to(inv, (own, 128))
    for n in range(9):
        w[rows_of(r), n * cin : (n + 1) * cin] = ((wraw[n].astype(F32) - centre) * inv).astype(BF)

    more = (r > 0) & (f % 2 == 0)
    fewer = jnp.logical_not(more)

    @pl.when(inside & more)
    def _():
        pl.semaphore_wait(bar, 6)

    @pl.when((inside & fewer) | (at_end & more))
    def _():
        pl.semaphore_wait(bar, 5)

    @pl.when(at_end & fewer)
    def _():
        pl.semaphore_wait(bar, 4)

    pairs = 2
    per = imgs // pairs
    order = [(row, h) for row in (1, 0) for h in range(pairs)]

    def piece_of(ref, j):
        row, h = order[j]
        return ref.at[slice(h * per, (h + 1) * per), row]

    def img_copy(j, k, to):
        return rc(piece_of(images, j), piece_of(raw.at[f], j), i_send.at[k, j], i_recv.at[f, j], to)

    def fwd_copy(j):
        slot = piece_of(raw.at[fq], j)
        return rc(slot, slot, i_send.at[2, j], i_recv.at[fq, j], p)

    def img_wait(t, j):
        wait_in(piece_of(raw.at[t], j), i_recv.at[t, j])

    c = f % 2
    share = rim_raw.at[pl.ds(c * per, per)]
    other = rim_raw.at[pl.ds((1 - c) * per, per)]
    rim_in = rc(images.at[pl.ds(c * per, per), 1], share, r_send.at[0], r_recv.at[0], below)
    rim_via = rc(raw.at[WIDE - 1, pl.ds(c * per, per), 1], share, r_send.at[0], r_recv.at[0], below)
    rim_to_p = rc(share, share, r_send.at[1], r_recv.at[1], p)

    for j in range(len(order)):
        img_copy(j, 1, q).start()

    @pl.when((f == 3) & (r < tall - 1))
    def _():
        rim_in.start()

    def w_copy(b, k, way):
        slot = w.at[rows_of(b), cols_of(k)]
        to = below if way == 0 else above
        return rc(slot, slot, w_send.at[way, b, k], w_recv.at[b, k], to)

    for k in range(PIECES):
        @pl.when(r < tall - 1)
        def _():
            w_copy(r, k, 0).start()

        @pl.when(r > 0)
        def _():
            w_copy(r, k, 1).start()

    for j in range(len(order)):
        img_copy(j, 0, p).start()

    def pass_on(s, k):
        up, dn = r - s, r + s

        @pl.when(inside & (up >= 0))
        def _():
            wait_in(w.at[rows_of(up), cols_of(k)], w_recv.at[up, k])
            w_copy(up, k, 0).start()

        @pl.when(inside & (dn <= tall - 1))
        def _():
            wait_in(w.at[rows_of(dn), cols_of(k)], w_recv.at[dn, k])
            w_copy(dn, k, 1).start()

    def w_wait_end(b):
        @pl.when(at_end)
        def _():
            for k in range(PIECES):
                wait_in(w.at[rows_of(b), cols_of(k)], w_recv.at[b, k])

    load_t.wait()
    want = goal_raw[...].reshape(px, goal_raw.shape[2])
    wide = goal_raw.shape[2]
    line = lax.broadcasted_iota(jnp.int32, (filters, wide), 0)
    chan = lax.broadcasted_iota(jnp.int32, (filters, wide), 1)
    first = (line // own) * (own * WIDE) + line % own
    for t in range(WIDE):
        pick = jnp.where(chan == first + t * own, 1.0, 0.0).astype(BF)
        goal[t] = dot(pick, want, NT).astype(BF)

    def half_rows(h):
        return pl.ds(pl.multiple_of(h * hf, hf), hf)

    def tgt_copy(b, k, to_f, to):
        return rc(
            goal.at[to_f, rows_of(b)], tg.at[f, rows_of(b)],
            t_send.at[k, b], t_recv.at[f, b], to,
        )

    def turn_block(it):
        return block(nth(jnp.where(it < 2, it + 1, jnp.where(it == 2, 0, it))))

    def tgt_across(it):
        b = turn_block(it)
        tgt_copy(b, 1, fq, q).start()
        tgt_copy(b, 2, fd, d).start()

    def tgt_wait(b):
        for t in (fq, fd):
            wait_in(tg.at[t, rows_of(b)], t_recv.at[t, b])

    near_half, far_half = flip, 1 - flip

    def tgt_near(b, carry):
        tgt_copy(b, 0, fp, p).start()
        return carry

    lax.fori_loop(0, tall, tgt_near, 0)
    tg[f] = goal[f]

    ii = lax.broadcasted_iota(jnp.int32, (2 * half, 2 * half), 0)
    jj = lax.broadcasted_iota(jnp.int32, (2 * half, 2 * half), 1)
    spread_out = jnp.where(jj == 2 * (ii % half) + ii // half, 1.0, 0.0).astype(BF)
    gather_in = jnp.where(ii == 2 * (jj % half) + jj // half, 1.0, 0.0).astype(BF)

    def split_one(index, at, block_img):
        v = dot(spread_out, block_img, NN).astype(BF)
        x[index, at : at + half, :one] = v[:half]
        x[index, at : at + half, one:] = v[half:]

    def split_pair(index, i0, a, b):
        split_one(index, i0 * half, a)
        split_one(index, (i0 + 1) * half, b)
        va = dot(a, gather_in, TN).astype(BF)
        vb = dot(b, gather_in, TN).astype(BF)
        lanes = slice(i0 * half, (i0 + 2) * half)
        xt[index, :one, lanes] = jnp.concatenate([va[:, :half], vb[:, :half]], axis=1)
        xt[index, one:, lanes] = jnp.concatenate([va[:, half:], vb[:, half:]], axis=1)

    def split_row(t, row):
        for i0 in range(0, imgs, 2):
            split_pair(1 + 2 * t + row, i0, raw[t, i0, row], raw[t, i0 + 1, row])

    def split_piece(t, j):
        row, h = order[j]
        for i0 in range(h * per, (h + 1) * per, 2):
            split_pair(1 + 2 * t + row, i0, raw[t, i0, row], raw[t, i0 + 1, row])

    def img_step(j):
        img_wait(fq, j)
        fwd_copy(j).start()

    def rim_step():
        @pl.when(r > 0)
        def _():
            wait_in(share, r_recv.at[0])
            rim_to_p.start()
            wait_in(other, r_recv.at[1])

    pass_on(1, 0)
    load_x.wait()
    for row in range(2):
        split_row(f, row)
    img_step(0)
    for j in range(len(order)):
        img_wait(fp, j)
    for row in range(2):
        split_row(fp, row)
    img_step(1)
    img_wait(fd, 0)
    img_wait(fd, 1)

    @pl.when((f < WIDE - 1) & (r < tall - 1))
    def _():
        rim_via.start()

    pass_on(1, 1)
    pass_on(1, 2)
    split_row(fq, 1)
    split_row(fd, 1)

    def tgt_near_wait(b, carry):
        wait_in(tg.at[fp, rows_of(b)], t_recv.at[fp, b])
        return carry

    lax.fori_loop(0, tall, tgt_near_wait, 0)

    place = lax.broadcasted_iota(jnp.int32, (own, px), 1) % half

    def forward(b, tiles):
        rows = rows_of(b)
        for t in tiles:
            even = jnp.zeros((own, px), F32)
            odd = jnp.zeros((2 * own, px), F32)
            for kh in range(3):
                c = kh * three
                even += dot(w[rows, c + one : c + two], xt[2 * t + kh, :one], NN)
                both = jnp.concatenate([w[rows, c + two : c + three], w[rows, c : c + one]], axis=0)
                odd += dot(both, xt[2 * t + kh, one:], NN)
            left = jnp.where(place == 0, 0.0, pltpu.roll(odd[own:], 1, 1))
            out = even + odd[:own] + left
            grad = ((out - tg[t, rows].astype(F32)) * GRAD_SCALE).astype(BF)
            nxt = jnp.where(place == half - 1, 0.0, pltpu.roll(grad.astype(F32), px - 1, 1))
            gt[t, rows] = grad
            gts[t, rows] = nxt.astype(BF)

    def filter_terms(b):
        rows = rows_of(b)
        lhs = [gt[t, rows] for t in range(WIDE)]
        both = [jnp.concatenate([gts[t, rows], lhs[t]], axis=0) for t in range(WIDE)]
        sums = jnp.zeros((own, one), F32)
        for kh in range(3):
            c = kh * three
            even = dot(lhs[0], x[kh, :, :one], NN)
            odd = dot(both[0], x[kh, :, one:], NN)
            for t in range(1, WIDE):
                even += dot(lhs[t], x[2 * t + kh, :, :one], NN)
                odd += dot(both[t], x[2 * t + kh, :, one:], NN)
            g[rows, c : c + one] = odd[:own]
            g[rows, c + one : c + two] = even
            g[rows, c + two : c + three] = odd[own:]
            sums += even + odd[:own] + odd[own:]
        mean = jnp.sum(sums, axis=1, keepdims=True) * (1.0 / fan)
        for n in range(9):
            lanes = slice(n * one, (n + 1) * one)
            g[rows, lanes] = g[rows, lanes] - mean

    def g_copy(way, b, k, to):
        at = (way, rows_of(b), strip_of(k))
        return rc(part_out.at[at], part_in.at[at], g_send.at[way, b, k], g_recv.at[way, b, k], to)

    def g_wait(way, b, k):
        wait_in(part_in.at[way, rows_of(b), strip_of(k)], g_recv.at[way, b, k])

    def g_first(b, k):
        rows, cols = rows_of(b), strip_of(k)
        part_out[flip, rows, cols] = g[rows, cols].astype(BF)
        g_copy(flip, b, k, ahead_dev).start()

    def g_relay(way, b, k, to):
        rows, cols = rows_of(b), strip_of(k)
        g_wait(way, b, k)
        part_out[way, rows, cols] = (g[rows, cols] + part_in[way, rows, cols].astype(F32)).astype(BF)
        g_copy(way, b, k, to).start()

    def relay_lead(n, k):
        @pl.when(inside & (n > u))
        def _():
            g_relay(flip, block(n), k, ahead_dev)

    def relay_trail(n, k):
        @pl.when(inside & (n < u))
        def _():
            g_relay(1 - flip, block(n), k, behind_dev)

    img_step(2)
    tgt_across(0)
    pass_on(2, 0)
    split_piece(fq, 2)
    img_wait(fd, 2)
    split_piece(fd, 2)
    rim_step()

    @pl.when(r > 0)
    def _():
        for i0 in range(0, imgs, 2):
            split_pair(0, i0, rim_raw[i0], rim_raw[i0 + 1])

    @pl.when(r == 0)
    def _():
        x[0] = jnp.zeros((px, two), BF)
        xt[0] = jnp.zeros((two, px), BF)

    first_b = block(u + 1)
    w_wait_end(first_b)
    img_step(3)

    def tgt_rest(it, carry):
        tgt_across(it)
        return carry

    lax.fori_loop(1, tall, tgt_rest, 0)
    pass_on(2, 1)
    forward(first_b, (f, fp))
    split_piece(fq, 3)
    img_wait(fd, 3)
    split_piece(fd, 3)
    pass_on(2, 2)
    for s in range(3, tall - 1):
        for k in range(PIECES):
            pass_on(s, k)

    def turn(it, carry):
        b = turn_block(it)
        n = block(b)

        @pl.when((it == 1) | (it > 2))
        def _():
            w_wait_end(b)

        @pl.when(it > 0)
        def _():
            forward(b, (f, fp))

        tgt_wait(b)
        forward(b, (fq, fd))

        @pl.when((it != 2) | at_end)
        def _():
            filter_terms(b)

        @pl.when(it == 1)
        def _():
            relay_lead(2, 0)

        @pl.when(at_end & (n == 1))
        def _():
            for k in range(START[0]):
                g_first(b, k)

            @pl.when(flip == 1)
            def _():
                for k in range(START[0], START[1]):
                    g_first(b, k)

        @pl.when(at_end & (n > 1))
        def _():
            for k in range(STRIPS):
                g_first(b, k)

        return carry

    lax.fori_loop(0, tall - 1, turn, 0)

    def turned(h):
        lanes = half_rows(h)
        for t in range(WIDE):
            gy[t, :, lanes] = gt[t, lanes].astype(F32).T.astype(BF)
            gys[t, :, lanes] = gts[t, lanes].astype(F32).T.astype(BF)

    gy[WIDE] = jnp.zeros((px, filters), BF)
    gys[WIDE] = jnp.zeros((px, filters), BF)
    turned(near_half)
    for k in range(1, 3):
        relay_lead(2, k)
    last_n = tall - 1
    last_b = block(last_n)
    w_wait_end(last_b)
    forward(last_b, (f, fp))
    tgt_wait(last_b)
    forward(last_b, (fq, fd))
    turned(far_half)
    for k in range(3, 6):
        relay_lead(2, k)

    def taps(t, kh):
        c = kh * three
        even = dot(gy[t], w[:, c + one : c + two], NN)
        odd = dot(gy[t], w[:, c + two : c + three], NN)
        odd += dot(gys[t], w[:, c : c + one], NN)
        return even, odd

    def tile_row(t, row):
        if row == 0:
            return taps(t, 1)
        even, odd = taps(t, 2)
        more_even, more_odd = taps(t + 1, 0)
        return even + more_even, odd + more_odd

    halves = (slice(0, one), slice(one, two))
    half_px = px // 2
    keep = pl.ds(pl.multiple_of(c * half_px, half_px), half_px)
    give = pl.ds(pl.multiple_of((1 - c) * half_px, half_px), half_px)
    rim_pc = rc(rim_x.at[give], rim_p, e_send.at[0], e_recv.at[0], p)
    rim_zc = rc(rim_s, rim_z.at[keep], e_send.at[1], e_recv.at[1 + c], above + 1 - c)

    def rim_zwait():
        for n in range(2):
            part = slice(n * half_px, (n + 1) * half_px)
            wait_in(rim_z.at[part], e_recv.at[1 + n])

    def p_copy(k, row):
        at = (k, row)
        return rc(to_p.at[at], from_p.at[at], d_send.at[at], d_recv.at[at], p)

    def q_copy(row):
        return rc(to_q.at[row], from_q.at[row], d_send.at[2, row], d_recv.at[2, row], q)

    def for_p(k, t):
        for row in range(2):
            for part, lanes in zip(tile_row(t, row), halves):
                to_p[k, row, :, lanes] = part.astype(BF)
            p_copy(k, row).start()

    def for_q(row):
        sums = tile_row(fq, row)
        wait_in(from_p.at[1, row], d_recv.at[1, row])
        for part, lanes in zip(sums, halves):
            acc[row, :, lanes] = part + from_p[1, row, :, lanes].astype(F32)

    @pl.when(r > 0)
    def _():
        edge = taps(0, 0)
        for part, lanes in zip(edge, halves):
            rim_x[:, lanes] = part.astype(BF)
        rim_pc.start()

    for_p(1, fd)
    for k in range(6, STRIPS):
        relay_lead(2, k)

    @pl.when(r > 0)
    def _():
        wait_in(rim_p, e_recv.at[0])
        rim_s[...] = (rim_x[keep].astype(F32) + rim_p[...].astype(F32)).astype(BF)
        rim_zc.start()

    filter_terms(last_b)

    @pl.when(at_end)
    def _():
        for k in range(STRIPS):
            g_first(last_b, k)

        @pl.when(flip == 0)
        def _():
            for k in range(START[0], START[1]):
                g_first(first_b, k)

        for k in range(START[1], STRIPS):
            g_first(first_b, k)

    for_q(0)
    to_q[0] = acc[0].astype(BF)
    q_copy(0).start()
    for_q(1)
    for_p(0, fp)

    @pl.when(inside)
    def _():
        filter_terms(block(u))

    relay_lead(3, 0)
    relay_lead(3, 1)

    @pl.when((f == 1) & (r < tall - 1))
    def _():
        rim_zwait()
        acc[1] += rim_z[...].astype(F32)

    to_q[1] = acc[1].astype(BF)
    q_copy(1).start()

    def both_ways(lag):
        for k in range(2, STRIPS + lag):
            if k < STRIPS:
                relay_lead(3, k)
            if k >= lag:
                relay_trail(tall - 4, k - lag)

    @pl.when(flip == 0)
    def _():
        both_ways(6)

    @pl.when(flip == 1)
    def _():
        both_ways(2)

    def relays(t, carry):
        for k in range(STRIPS):
            relay_lead(t, k)
            relay_trail(tall - 1 - t, k)
        return carry

    if tall > 4:
        lax.fori_loop(4, tall, relays, 0)

    for row in range(2):
        for part, lanes in zip(tile_row(f, row), halves):
            acc[row, :, lanes] = part
        wait_in(from_p.at[0, row], d_recv.at[0, row])
        acc[row] += from_p[0, row].astype(F32)

    @pl.when((r < tall - 1) & (f == 3))
    def _():
        rim_zwait()
        acc[1] += rim_z[...].astype(F32)

    def finish_row(row):
        wait_in(from_q.at[row], d_recv.at[2, row])
        total = (acc[row] + from_q[row].astype(F32)).astype(BF)
        for i in range(imgs):
            mine = total[i * half : (i + 1) * half]
            stacked = jnp.concatenate([mine[:, :one], mine[:, one:]], axis=0)
            dout[i, row] = dot(gather_in, stacked, NN).astype(BF)

    finish_row(0)
    finish_row(1)

    mine = rows_of(r)
    centre = stat[0][:, :1]
    inv = stat[1][:, :1]
    s1 = jnp.zeros((own, cin), F32)
    s2 = jnp.zeros((own, cin), F32)
    for k in range(STRIPS):
        cols = strip_of(k)

        @pl.when(r > 0)
        def _():
            g_wait(0, r, k)
            g[mine, cols] += part_in[0, mine, cols].astype(F32)

        @pl.when(r < tall - 1)
        def _():
            g_wait(1, r, k)
            g[mine, cols] += part_in[1, mine, cols].astype(F32)

        piece = g[mine, cols]
        s1 += piece
        s2 += piece * ((wraw[k].astype(F32) - centre) * inv)
    m1 = jnp.sum(s1, axis=1, keepdims=True) * (1.0 / fan)
    m2 = jnp.sum(s2, axis=1, keepdims=True) * (1.0 / fan)
    for n in range(9):
        hat = (wraw[n].astype(F32) - centre) * inv
        gout[n] = (g[mine, strip_of(n)] - m1 - hat * m2) * inv

    for j in range(len(order)):
        img_copy(j, 0, p).wait_send()
        img_copy(j, 1, q).wait_send()
        fwd_copy(j).wait_send()
    for row in range(2):
        p_copy(0, row).wait_send()
        p_copy(1, row).wait_send()
        q_copy(row).wait_send()

    @pl.when(r < tall - 1)
    def _():
        rim_in.wait_send()

    @pl.when(r > 0)
    def _():
        rim_to_p.wait_send()

    @pl.when(r > 0)
    def _():
        rim_pc.wait_send()
        rim_zc.wait_send()

    def drain(b, carry):
        tgt_copy(b, 0, fp, p).wait_send()
        tgt_copy(b, 1, fq, q).wait_send()
        tgt_copy(b, 2, fd, d).wait_send()
        for k in range(PIECES):
            @pl.when((r < tall - 1) & (b <= r))
            def _():
                w_copy(b, k, 0).wait_send()

            @pl.when((r > 0) & (b >= r))
            def _():
                w_copy(b, k, 1).wait_send()

        for k in range(STRIPS):
            @pl.when(b > r)
            def _():
                g_copy(0, b, k, p).wait_send()

            @pl.when(b < r)
            def _():
                g_copy(1, b, k, p).wait_send()

        return carry

    lax.fori_loop(0, tall, drain, 0)


def shards(images, target, raw_filters):
    imgs, two_rows, in_cols, cin = images.shape
    half = in_cols // 2
    own = raw_filters.shape[0]
    tall = lax.axis_size("space") // WIDE
    fan = 9 * cin
    px = imgs * half
    filters = tall * own
    wide = target.shape[3]
    vm = pltpu.VMEM
    dma = pltpu.SemaphoreType.DMA
    row = (px, 2 * cin)
    scratch = [
        vm((WIDE,) + images.shape, BF), vm((imgs, in_cols, cin), BF), vm((imgs, half, wide), BF),
        vm((9, own, cin), BF), vm((2, own, 128), F32),
        vm((2 * WIDE + 1,) + row, BF), vm((2 * WIDE + 1, 2 * cin, px), BF), vm((filters, fan), BF),
        vm((WIDE, filters, px), BF), vm((WIDE, filters, px), BF),
        vm((WIDE + 1, px, filters), BF), vm((WIDE + 1, px, filters), BF),
        vm((WIDE, filters, px), BF), vm((WIDE, filters, px), BF), vm((filters, fan), F32),
        vm((2, filters, fan), BF), vm((2, filters, fan), BF),
        vm((2, 2) + row, BF), vm((2, 2) + row, BF), vm((2,) + row, BF), vm((2,) + row, BF),
        vm((2,) + row, F32),
        vm(row, BF), vm((px // 2, 2 * cin), BF), vm((px // 2, 2 * cin), BF), vm(row, BF),
        dma((3,)), dma((WIDE, 4)), dma((3, 4)), dma((tall, PIECES)), dma((2, tall, PIECES)),
        dma((WIDE, tall)), dma((3, tall)), dma((2,)), dma((2,)),
        dma((2, tall, STRIPS)), dma((2, tall, STRIPS)), dma((3, 2)), dma((3, 2)), dma((3,)), dma((2,)),
    ]
    input_grads, by_tap = pl.pallas_call(
        functools.partial(kernel, tall, own, half, cin),
        out_shape=(
            pltpu.VMEM(images.shape, BF),
            pltpu.VMEM((9, own, cin), F32),
        ),
        in_specs=[pl.BlockSpec(memory_space=pl.ANY)] * 3,
        out_specs=[pl.BlockSpec(memory_space=pltpu.VMEM)] * 2,
        scratch_shapes=scratch,
        compiler_params=pltpu.CompilerParams(
            collective_id=0, has_side_effects=True, vmem_limit_bytes=56 * 1024 * 1024
        ),
        name="tiles",
    )(
        images,
        target.reshape(imgs, half, wide),
        raw_filters.transpose(1, 2, 0, 3).reshape(9, own, cin),
    )
    filter_grads = by_tap.reshape(3, 3, own, cin).transpose(2, 0, 1, 3)
    return (input_grads, filter_grads)


def solution(mesh):
    return jax.shard_map(
        shards,
        mesh=mesh,
        in_specs=(
            P("parts", "space", None, None),
            P("parts", "space", None, None),
            P(("parts", "space"), None, None, None),
        ),
        out_specs=(P("parts", "space", None, None), P(("parts", "space"), None, None, None)),
        check_vma=False,
    )
```

```python
import functools

import jax
import jax.numpy as jnp
from jax import lax
from jax.experimental import pallas as pl
from jax.experimental.pallas import tpu as pltpu
from jax.sharding import PartitionSpec as P

EPS = 1e-05
GRAD_SCALE = 0.015625
WIDE = 4
PIECES = 3
STRIPS = 9
START = (2, 3)
F32 = jnp.float32
BF = jnp.bfloat16
NT = (((1,), (1,)), ((), ()))
NN = (((1,), (0,)), ((), ()))
TN = (((0,), (0,)), ((), ()))
MESH = pl.DeviceIdType.MESH


def dot(a, b, dims):
    return lax.dot_general(a, b, dims, preferred_element_type=F32)


def kernel(
    tall, own, half, cin,
    images, target, filters_in, dout, gout,
    raw, rim_raw, goal_raw, wraw, stat,
    x, xt, w, goal, tg, gy, gys, gt, gts, g, part_in, part_out,
    to_p, from_p, to_q, from_q, acc, rim_x, rim_p, rim_s, rim_z,
    l_sem, i_recv, i_send, w_recv, w_send, t_recv, t_send, r_recv, r_send,
    g_recv, g_send, d_recv, d_send, e_recv, e_send,
):
    me = lax.axis_index("space")
    r, f = me // WIDE, me % WIDE
    base = r * WIDE
    fp = f + 1 - 2 * (f % 2)
    fq = f + 2 - 4 * (f // 2)
    fd = fp + 2 - 4 * (fp // 2)
    p, q, d = base + fp, base + fq, base + fd
    above, below = me - WIDE, me + WIDE
    imgs = images.shape[0]
    px = imgs * half
    two, one = 2 * cin, cin
    three = 3 * cin
    filters = tall * own
    fan = 9 * cin
    mid = tall // 2
    hf = filters // 2
    flip = r // mid
    u = r + flip * (tall - 1 - 2 * r)
    ahead_dev = me + WIDE - 2 * WIDE * flip
    behind_dev = me - WIDE + 2 * WIDE * flip
    at_end = u == 0
    inside = u > 0

    def rc(src, dst, ssem, rsem, to):
        return pltpu.make_async_remote_copy(
            src_ref=src, dst_ref=dst, send_sem=ssem, recv_sem=rsem,
            device_id={"space": to}, device_id_type=MESH,
        )

    def wait_in(dst, rsem):
        rc(dst, dst, rsem, rsem, p).wait_recv()

    def rows_of(b):
        return pl.ds(pl.multiple_of(b * own, own), own)

    wide_cols = fan // PIECES

    def cols_of(k):
        return slice(k * wide_cols, (k + 1) * wide_cols)

    strip_cols = fan // STRIPS

    def strip_of(k):
        return slice(k * strip_cols, (k + 1) * strip_cols)

    def block(n):
        return n + flip * (tall - 1 - 2 * n)

    def nth(i):
        near = jnp.where(i % 2 == 1, u + (i + 1) // 2, u - i // 2)
        return jnp.where(i > 2 * u, i, near)

    bar = pltpu.get_barrier_semaphore()

    def greet(to):
        pl.semaphore_signal(bar, inc=1, device_id={"space": to}, device_id_type=MESH)

    for to in (p, q, d):
        greet(to)

    @pl.when(r > 0)
    def _():
        greet(above)

    @pl.when(r < tall - 1)
    def _():
        greet(below)

    load_w = pltpu.make_async_copy(filters_in, wraw, l_sem.at[0])
    load_x = pltpu.make_async_copy(images, raw.at[f], l_sem.at[1])
    load_t = pltpu.make_async_copy(target, goal_raw, l_sem.at[2])
    load_w.start()
    load_x.start()
    load_t.start()

    @pl.when((r < tall - 1) & (f % 2 == 1))
    def _():
        greet(below - 1)

    load_w.wait()
    centre = wraw[0].astype(F32)
    for k in range(1, 9):
        centre += wraw[k].astype(F32)
    centre = jnp.sum(centre, axis=1, keepdims=True) * (1.0 / fan)
    spread = jnp.zeros((own, cin), F32)
    for k in range(9):
        off = wraw[k].astype(F32) - centre
        spread += off * off
    spread = jnp.sqrt(jnp.sum(spread, axis=1, keepdims=True) * (1.0 / fan) + EPS)
    inv = 1.0 / spread
    stat[0] = jnp.broadcast_to(centre, (own, 128))
    stat[1] = jnp.broadcast_to(inv, (own, 128))
    for n in range(9):
        w[rows_of(r), n * cin : (n + 1) * cin] = ((wraw[n].astype(F32) - centre) * inv).astype(BF)

    more = (r > 0) & (f % 2 == 0)
    fewer = jnp.logical_not(more)

    @pl.when(inside & more)
    def _():
        pl.semaphore_wait(bar, 6)

    @pl.when((inside & fewer) | (at_end & more))
    def _():
        pl.semaphore_wait(bar, 5)

    @pl.when(at_end & fewer)
    def _():
        pl.semaphore_wait(bar, 4)

    pairs = 2
    per = imgs // pairs
    order = [(row, h) for row in (1, 0) for h in range(pairs)]

    def piece_of(ref, j):
        row, h = order[j]
        return ref.at[slice(h * per, (h + 1) * per), row]

    def img_copy(j, k, to):
        return rc(piece_of(images, j), piece_of(raw.at[f], j), i_send.at[k, j], i_recv.at[f, j], to)

    def fwd_copy(j):
        slot = piece_of(raw.at[fq], j)
        return rc(slot, slot, i_send.at[2, j], i_recv.at[fq, j], p)

    def img_wait(t, j):
        wait_in(piece_of(raw.at[t], j), i_recv.at[t, j])

    c = f % 2
    share = rim_raw.at[pl.ds(c * per, per)]
    other = rim_raw.at[pl.ds((1 - c) * per, per)]
    rim_in = rc(images.at[pl.ds(c * per, per), 1], share, r_send.at[0], r_recv.at[0], below)
    rim_via = rc(raw.at[WIDE - 1, pl.ds(c * per, per), 1], share, r_send.at[0], r_recv.at[0], below)
    rim_to_p = rc(share, share, r_send.at[1], r_recv.at[1], p)

    for j in range(len(order)):
        img_copy(j, 1, q).start()

    @pl.when((f == 3) & (r < tall - 1))
    def _():
        rim_in.start()

    def w_copy(b, k, way):
        slot = w.at[rows_of(b), cols_of(k)]
        to = below if way == 0 else above
        return rc(slot, slot, w_send.at[way, b, k], w_recv.at[b, k], to)

    for k in range(PIECES):
        @pl.when(r < tall - 1)
        def _():
            w_copy(r, k, 0).start()

        @pl.when(r > 0)
        def _():
            w_copy(r, k, 1).start()

    for j in range(len(order)):
        img_copy(j, 0, p).start()

    def pass_on(s, k):
        up, dn = r - s, r + s

        @pl.when(inside & (up >= 0))
        def _():
            wait_in(w.at[rows_of(up), cols_of(k)], w_recv.at[up, k])
            w_copy(up, k, 0).start()

        @pl.when(inside & (dn <= tall - 1))
        def _():
            wait_in(w.at[rows_of(dn), cols_of(k)], w_recv.at[dn, k])
            w_copy(dn, k, 1).start()

    def w_wait_end(b):
        @pl.when(at_end)
        def _():
            for k in range(PIECES):
                wait_in(w.at[rows_of(b), cols_of(k)], w_recv.at[b, k])

    load_t.wait()
    want = goal_raw[...].reshape(px, goal_raw.shape[2])
    wide = goal_raw.shape[2]
    line = lax.broadcasted_iota(jnp.int32, (filters, wide), 0)
    chan = lax.broadcasted_iota(jnp.int32, (filters, wide), 1)
    first = (line // own) * (own * WIDE) + line % own
    for t in range(WIDE):
        pick = jnp.where(chan == first + t * own, 1.0, 0.0).astype(BF)
        goal[t] = dot(pick, want, NT).astype(BF)

    def half_rows(h):
        return pl.ds(pl.multiple_of(h * hf, hf), hf)

    def tgt_copy(h, k, to_f, to):
        return rc(
            goal.at[to_f, half_rows(h)], tg.at[f, half_rows(h)],
            t_send.at[k, h], t_recv.at[f, h], to,
        )

    near_half, far_half = flip, 1 - flip
    crossing = (u + 1) // mid
    soon = flip + crossing * (1 - 2 * flip)
    later = 1 - soon
    tgt_copy(soon, 0, fp, p).start()
    tgt_copy(later, 0, fp, p).start()
    tg[f] = goal[f]

    ii = lax.broadcasted_iota(jnp.int32, (2 * half, 2 * half), 0)
    jj = lax.broadcasted_iota(jnp.int32, (2 * half, 2 * half), 1)
    spread_out = jnp.where(jj == 2 * (ii % half) + ii // half, 1.0, 0.0).astype(BF)
    gather_in = jnp.where(ii == 2 * (jj % half) + jj // half, 1.0, 0.0).astype(BF)

    def split_one(index, at, block_img):
        v = dot(spread_out, block_img, NN).astype(BF)
        x[index, at : at + half, :one] = v[:half]
        x[index, at : at + half, one:] = v[half:]

    def split_pair(index, i0, a, b):
        split_one(index, i0 * half, a)
        split_one(index, (i0 + 1) * half, b)
        va = dot(a, gather_in, TN).astype(BF)
        vb = dot(b, gather_in, TN).astype(BF)
        lanes = slice(i0 * half, (i0 + 2) * half)
        xt[index, :one, lanes] = jnp.concatenate([va[:, :half], vb[:, :half]], axis=1)
        xt[index, one:, lanes] = jnp.concatenate([va[:, half:], vb[:, half:]], axis=1)

    def split_row(t, row):
        for i0 in range(0, imgs, 2):
            split_pair(1 + 2 * t + row, i0, raw[t, i0, row], raw[t, i0 + 1, row])

    def img_step(j):
        img_wait(fq, j)
        fwd_copy(j).start()

    def rim_step():
        @pl.when(r > 0)
        def _():
            wait_in(share, r_recv.at[0])
            rim_to_p.start()
            wait_in(other, r_recv.at[1])

    pass_on(1, 0)
    load_x.wait()
    for row in range(2):
        split_row(f, row)
    img_step(0)
    for j in range(len(order)):
        img_wait(fp, j)
    for row in range(2):
        split_row(fp, row)
    img_step(1)
    img_wait(fd, 0)
    img_wait(fd, 1)

    @pl.when((f < WIDE - 1) & (r < tall - 1))
    def _():
        rim_via.start()

    pass_on(1, 1)
    pass_on(1, 2)
    split_row(fq, 1)
    split_row(fd, 1)
    for h in range(2):
        wait_in(tg.at[fp, half_rows(h)], t_recv.at[fp, h])

    place = lax.broadcasted_iota(jnp.int32, (own, px), 1) % half

    def forward(b, tiles):
        rows = rows_of(b)
        for t in tiles:
            even = jnp.zeros((own, px), F32)
            odd = jnp.zeros((2 * own, px), F32)
            for kh in range(3):
                c = kh * three
                even += dot(w[rows, c + one : c + two], xt[2 * t + kh, :one], NN)
                both = jnp.concatenate([w[rows, c + two : c + three], w[rows, c : c + one]], axis=0)
                odd += dot(both, xt[2 * t + kh, one:], NN)
            left = jnp.where(place == 0, 0.0, pltpu.roll(odd[own:], 1, 1))
            out = even + odd[:own] + left
            grad = ((out - tg[t, rows].astype(F32)) * GRAD_SCALE).astype(BF)
            nxt = jnp.where(place == half - 1, 0.0, pltpu.roll(grad.astype(F32), px - 1, 1))
            gt[t, rows] = grad
            gts[t, rows] = nxt.astype(BF)

    def filter_terms(b):
        rows = rows_of(b)
        lhs = [gt[t, rows] for t in range(WIDE)]
        both = [jnp.concatenate([gts[t, rows], lhs[t]], axis=0) for t in range(WIDE)]
        sums = jnp.zeros((own, one), F32)
        for kh in range(3):
            c = kh * three
            even = dot(lhs[0], x[kh, :, :one], NN)
            odd = dot(both[0], x[kh, :, one:], NN)
            for t in range(1, WIDE):
                even += dot(lhs[t], x[2 * t + kh, :, :one], NN)
                odd += dot(both[t], x[2 * t + kh, :, one:], NN)
            g[rows, c : c + one] = odd[:own]
            g[rows, c + one : c + two] = even
            g[rows, c + two : c + three] = odd[own:]
            sums += even + odd[:own] + odd[own:]
        mean = jnp.sum(sums, axis=1, keepdims=True) * (1.0 / fan)
        for n in range(9):
            lanes = slice(n * one, (n + 1) * one)
            g[rows, lanes] = g[rows, lanes] - mean

    def g_copy(way, b, k, to):
        at = (way, rows_of(b), strip_of(k))
        return rc(part_out.at[at], part_in.at[at], g_send.at[way, b, k], g_recv.at[way, b, k], to)

    def g_wait(way, b, k):
        wait_in(part_in.at[way, rows_of(b), strip_of(k)], g_recv.at[way, b, k])

    def g_first(b, k):
        rows, cols = rows_of(b), strip_of(k)
        part_out[flip, rows, cols] = g[rows, cols].astype(BF)
        g_copy(flip, b, k, ahead_dev).start()

    def g_relay(way, b, k, to):
        rows, cols = rows_of(b), strip_of(k)
        g_wait(way, b, k)
        part_out[way, rows, cols] = (g[rows, cols] + part_in[way, rows, cols].astype(F32)).astype(BF)
        g_copy(way, b, k, to).start()

    def relay_lead(n, k):
        @pl.when(inside & (n > u))
        def _():
            g_relay(flip, block(n), k, ahead_dev)

    def relay_trail(n, k):
        @pl.when(inside & (n < u))
        def _():
            g_relay(1 - flip, block(n), k, behind_dev)

    img_step(2)
    for k, (to_f, to) in ((1, (fq, q)), (2, (fd, d))):
        tgt_copy(soon, k, to_f, to).start()
    pass_on(2, 0)
    rim_step()

    @pl.when(r > 0)
    def _():
        for i0 in range(0, imgs, 2):
            split_pair(0, i0, rim_raw[i0], rim_raw[i0 + 1])

    @pl.when(r == 0)
    def _():
        x[0] = jnp.zeros((px, two), BF)
        xt[0] = jnp.zeros((two, px), BF)

    first_b = block(u + 1)
    w_wait_end(first_b)
    img_step(3)
    for k, (to_f, to) in ((1, (fq, q)), (2, (fd, d))):
        tgt_copy(later, k, to_f, to).start()
    pass_on(2, 1)
    forward(first_b, (f, fp))
    split_row(fq, 0)
    img_wait(fd, 2)
    img_wait(fd, 3)
    split_row(fd, 0)
    pass_on(2, 2)
    for s in range(3, tall - 1):
        for k in range(PIECES):
            pass_on(s, k)
    for t in (fq, fd):
        wait_in(tg.at[t, half_rows(soon)], t_recv.at[t, soon])

    def turn(it, carry):
        i = jnp.where(it < 2, it + 1, jnp.where(it == 2, 0, it))
        n = nth(i)
        b = block(n)

        @pl.when((it == 1) | (it > 2))
        def _():
            w_wait_end(b)

        @pl.when(it == 1)
        def _():
            for t in (fq, fd):
                wait_in(tg.at[t, half_rows(later)], t_recv.at[t, later])

        @pl.when(it > 0)
        def _():
            forward(b, (f, fp))

        forward(b, (fq, fd))
        filter_terms(b)

        @pl.when(at_end & (n == 1))
        def _():
            for k in range(START[0]):
                g_first(b, k)

            @pl.when(flip == 1)
            def _():
                for k in range(START[0], START[1]):
                    g_first(b, k)

        @pl.when(at_end & (n > 1))
        def _():
            for k in range(STRIPS):
                g_first(b, k)

        return carry

    lax.fori_loop(0, tall - 1, turn, 0)

    def turned(h):
        lanes = half_rows(h)
        for t in range(WIDE):
            gy[t, :, lanes] = gt[t, lanes].astype(F32).T.astype(BF)
            gys[t, :, lanes] = gts[t, lanes].astype(F32).T.astype(BF)

    gy[WIDE] = jnp.zeros((px, filters), BF)
    gys[WIDE] = jnp.zeros((px, filters), BF)
    turned(near_half)
    for k in range(3):
        relay_lead(2, k)
    last_n = tall - 1
    last_b = block(last_n)
    w_wait_end(last_b)
    forward(last_b, (f, fp))
    forward(last_b, (fq, fd))
    turned(far_half)
    for k in range(3, 6):
        relay_lead(2, k)

    def taps(t, kh):
        c = kh * three
        even = dot(gy[t], w[:, c + one : c + two], NN)
        odd = dot(gy[t], w[:, c + two : c + three], NN)
        odd += dot(gys[t], w[:, c : c + one], NN)
        return even, odd

    def tile_row(t, row):
        if row == 0:
            return taps(t, 1)
        even, odd = taps(t, 2)
        more_even, more_odd = taps(t + 1, 0)
        return even + more_even, odd + more_odd

    halves = (slice(0, one), slice(one, two))
    half_px = px // 2
    keep = pl.ds(pl.multiple_of(c * half_px, half_px), half_px)
    give = pl.ds(pl.multiple_of((1 - c) * half_px, half_px), half_px)
    rim_pc = rc(rim_x.at[give], rim_p, e_send.at[0], e_recv.at[0], p)
    rim_zc = rc(rim_s, rim_z.at[keep], e_send.at[1], e_recv.at[1 + c], above + 1 - c)

    def rim_zwait():
        for n in range(2):
            part = slice(n * half_px, (n + 1) * half_px)
            wait_in(rim_z.at[part], e_recv.at[1 + n])

    def p_copy(k, row):
        at = (k, row)
        return rc(to_p.at[at], from_p.at[at], d_send.at[at], d_recv.at[at], p)

    def q_copy(row):
        return rc(to_q.at[row], from_q.at[row], d_send.at[2, row], d_recv.at[2, row], q)

    def for_p(k, t):
        for row in range(2):
            for part, lanes in zip(tile_row(t, row), halves):
                to_p[k, row, :, lanes] = part.astype(BF)
            p_copy(k, row).start()

    def for_q(row):
        sums = tile_row(fq, row)
        wait_in(from_p.at[1, row], d_recv.at[1, row])
        for part, lanes in zip(sums, halves):
            acc[row, :, lanes] = part + from_p[1, row, :, lanes].astype(F32)

    @pl.when(r > 0)
    def _():
        edge = taps(0, 0)
        for part, lanes in zip(edge, halves):
            rim_x[:, lanes] = part.astype(BF)
        rim_pc.start()

    for_p(1, fd)
    for k in range(6, STRIPS):
        relay_lead(2, k)

    @pl.when(r > 0)
    def _():
        wait_in(rim_p, e_recv.at[0])
        rim_s[...] = (rim_x[keep].astype(F32) + rim_p[...].astype(F32)).astype(BF)
        rim_zc.start()

    filter_terms(last_b)

    @pl.when(at_end)
    def _():
        for k in range(STRIPS):
            g_first(last_b, k)

        @pl.when(flip == 0)
        def _():
            for k in range(START[0], START[1]):
                g_first(first_b, k)

        for k in range(START[1], STRIPS):
            g_first(first_b, k)

    for_q(0)
    to_q[0] = acc[0].astype(BF)
    q_copy(0).start()
    for_q(1)
    for_p(0, fp)
    relay_lead(3, 0)
    relay_lead(3, 1)

    @pl.when((f == 1) & (r < tall - 1))
    def _():
        rim_zwait()
        acc[1] += rim_z[...].astype(F32)

    to_q[1] = acc[1].astype(BF)
    q_copy(1).start()

    def both_ways(lag):
        for k in range(2, STRIPS + lag):
            if k < STRIPS:
                relay_lead(3, k)
            if k >= lag:
                relay_trail(tall - 4, k - lag)

    @pl.when(flip == 0)
    def _():
        both_ways(6)

    @pl.when(flip == 1)
    def _():
        both_ways(2)

    def relays(t, carry):
        for k in range(STRIPS):
            relay_lead(t, k)
            relay_trail(tall - 1 - t, k)
        return carry

    if tall > 4:
        lax.fori_loop(4, tall, relays, 0)

    for row in range(2):
        for part, lanes in zip(tile_row(f, row), halves):
            acc[row, :, lanes] = part
        wait_in(from_p.at[0, row], d_recv.at[0, row])
        acc[row] += from_p[0, row].astype(F32)

    @pl.when((r < tall - 1) & (f == 3))
    def _():
        rim_zwait()
        acc[1] += rim_z[...].astype(F32)

    def finish_row(row):
        wait_in(from_q.at[row], d_recv.at[2, row])
        total = (acc[row] + from_q[row].astype(F32)).astype(BF)
        for i in range(imgs):
            mine = total[i * half : (i + 1) * half]
            stacked = jnp.concatenate([mine[:, :one], mine[:, one:]], axis=0)
            dout[i, row] = dot(gather_in, stacked, NN).astype(BF)

    finish_row(0)
    finish_row(1)

    mine = rows_of(r)
    centre = stat[0][:, :1]
    inv = stat[1][:, :1]
    s1 = jnp.zeros((own, cin), F32)
    s2 = jnp.zeros((own, cin), F32)
    for k in range(STRIPS):
        cols = strip_of(k)

        @pl.when(r > 0)
        def _():
            g_wait(0, r, k)
            g[mine, cols] += part_in[0, mine, cols].astype(F32)

        @pl.when(r < tall - 1)
        def _():
            g_wait(1, r, k)
            g[mine, cols] += part_in[1, mine, cols].astype(F32)

        piece = g[mine, cols]
        s1 += piece
        s2 += piece * ((wraw[k].astype(F32) - centre) * inv)
    m1 = jnp.sum(s1, axis=1, keepdims=True) * (1.0 / fan)
    m2 = jnp.sum(s2, axis=1, keepdims=True) * (1.0 / fan)
    for n in range(9):
        hat = (wraw[n].astype(F32) - centre) * inv
        gout[n] = (g[mine, strip_of(n)] - m1 - hat * m2) * inv

    for j in range(len(order)):
        img_copy(j, 0, p).wait_send()
        img_copy(j, 1, q).wait_send()
        fwd_copy(j).wait_send()
    for h in range(2):
        tgt_copy(h, 0, fp, p).wait_send()
        tgt_copy(h, 1, fq, q).wait_send()
        tgt_copy(h, 2, fd, d).wait_send()
    for row in range(2):
        p_copy(0, row).wait_send()
        p_copy(1, row).wait_send()
        q_copy(row).wait_send()

    @pl.when(r < tall - 1)
    def _():
        rim_in.wait_send()

    @pl.when(r > 0)
    def _():
        rim_to_p.wait_send()

    @pl.when(r > 0)
    def _():
        rim_pc.wait_send()
        rim_zc.wait_send()

    def drain(b, carry):
        for k in range(PIECES):
            @pl.when((r < tall - 1) & (b <= r))
            def _():
                w_copy(b, k, 0).wait_send()

            @pl.when((r > 0) & (b >= r))
            def _():
                w_copy(b, k, 1).wait_send()

        for k in range(STRIPS):
            @pl.when(b > r)
            def _():
                g_copy(0, b, k, p).wait_send()

            @pl.when(b < r)
            def _():
                g_copy(1, b, k, p).wait_send()

        return carry

    lax.fori_loop(0, tall, drain, 0)


def shards(images, target, raw_filters):
    imgs, two_rows, in_cols, cin = images.shape
    half = in_cols // 2
    own = raw_filters.shape[0]
    tall = lax.axis_size("space") // WIDE
    fan = 9 * cin
    px = imgs * half
    filters = tall * own
    wide = target.shape[3]
    vm = pltpu.VMEM
    dma = pltpu.SemaphoreType.DMA
    row = (px, 2 * cin)
    scratch = [
        vm((WIDE,) + images.shape, BF), vm((imgs, in_cols, cin), BF), vm((imgs, half, wide), BF),
        vm((9, own, cin), BF), vm((2, own, 128), F32),
        vm((2 * WIDE + 1,) + row, BF), vm((2 * WIDE + 1, 2 * cin, px), BF), vm((filters, fan), BF),
        vm((WIDE, filters, px), BF), vm((WIDE, filters, px), BF),
        vm((WIDE + 1, px, filters), BF), vm((WIDE + 1, px, filters), BF),
        vm((WIDE, filters, px), BF), vm((WIDE, filters, px), BF), vm((filters, fan), F32),
        vm((2, filters, fan), BF), vm((2, filters, fan), BF),
        vm((2, 2) + row, BF), vm((2, 2) + row, BF), vm((2,) + row, BF), vm((2,) + row, BF),
        vm((2,) + row, F32),
        vm(row, BF), vm((px // 2, 2 * cin), BF), vm((px // 2, 2 * cin), BF), vm(row, BF),
        dma((3,)), dma((WIDE, 4)), dma((3, 4)), dma((tall, PIECES)), dma((2, tall, PIECES)),
        dma((WIDE, 2)), dma((3, 2)), dma((2,)), dma((2,)),
        dma((2, tall, STRIPS)), dma((2, tall, STRIPS)), dma((3, 2)), dma((3, 2)), dma((3,)), dma((2,)),
    ]
    input_grads, by_tap = pl.pallas_call(
        functools.partial(kernel, tall, own, half, cin),
        out_shape=(
            pltpu.VMEM(images.shape, BF),
            pltpu.VMEM((9, own, cin), F32),
        ),
        in_specs=[pl.BlockSpec(memory_space=pl.ANY)] * 3,
        out_specs=[pl.BlockSpec(memory_space=pltpu.VMEM)] * 2,
        scratch_shapes=scratch,
        compiler_params=pltpu.CompilerParams(
            collective_id=0, has_side_effects=True, vmem_limit_bytes=56 * 1024 * 1024
        ),
        name="tiles",
    )(
        images,
        target.reshape(imgs, half, wide),
        raw_filters.transpose(1, 2, 0, 3).reshape(9, own, cin),
    )
    filter_grads = by_tap.reshape(3, 3, own, cin).transpose(2, 0, 1, 3)
    return (input_grads, filter_grads)


def solution(mesh):
    return jax.shard_map(
        shards,
        mesh=mesh,
        in_specs=(
            P("parts", "space", None, None),
            P("parts", "space", None, None),
            P(("parts", "space"), None, None, None),
        ),
        out_specs=(P("parts", "space", None, None), P(("parts", "space"), None, None, None)),
        check_vma=False,
    )
```
